128 devices in a mesh: ctx: 16 (over y_hi, x, core), head: 8 (over z, y_lo).
Axes of the slice: x: 4, y: 4 (y_hi: 2, y_lo: 2; y = y_hi * 2 + y_lo), z: 4, core: 2. Of those that a mesh axis runs over, the one named last changes fastest.
Arguments:
- queries: bfloat16 [4096, 4096], P('ctx', 'head'), may hold values from -80 to 80
- keys: bfloat16 [4096, 2048], P('ctx', 'head'), may hold values from -6 to 6
- values: bfloat16 [4096, 2048], P('ctx', 'head'), may hold values from -6 to 6
- grad_out: bfloat16 [4096, 4096], P('ctx', 'head'), may hold values from -6 to 6
- chosen: int32 [64, 16, 16], P('ctx', 'head'), may hold values from 0 to 63, as said below
- w_query: bfloat16 [4608, 4096], P(None, 'head'), may hold values from -0.09375 to 0.09375
- w_key: bfloat16 [4608, 2048], P(None, 'head'), may hold values from -0.09375 to 0.09375
- w_value: bfloat16 [4608, 2048], P(None, 'head'), may hold values from -0.09375 to 0.09375
Outputs:
- grad_queries: bfloat16 [4096, 4096], P('ctx', 'head')
- grad_keys: bfloat16 [4096, 2048], P('ctx', 'head')
- grad_values: bfloat16 [4096, 2048], P('ctx', 'head')
- grad_input: bfloat16 [4096, 4608], P('ctx', 'head')
The draws below stay inside these ranges and needn't reach their ends.
Inputs may be any that keep to these rules, and one draw needn't show every extreme that they name: `chosen`: each list names 16 different blocks; it always names block 0 and the query's own block, and a query block b below 16 names every block 0 .. b; entries above the query's own block contribute no keys.
All inputs are finite; a program needn't handle non-finite values.
Results may differ from the reference program's by a relative error of at most 0.019.
Values may be sent and summed in bfloat16 or wider, within the bound.
A program may use at most 128 MiB of HBM per device.

```python
import math
import jax
import jax.numpy as jnp
from jax import lax

D = 4608
HEADS = 32
GROUPS = 16
HEAD_DIM = 128
BLOCK = 64
TOPK = 16
TOK_DEV = 256
TOKENS = 4096
NBLK = 64
N_CTX = 16
N_HEAD = 8


def joint_fields(key):
    base_key = jax.random.fold_in(key, 11)
    k_keys = jax.random.fold_in(base_key, 0)
    k_query = jax.random.fold_in(base_key, 3)
    key_field = jax.random.truncated_normal(k_keys, -6.0, 6.0, (TOKENS, GROUPS * HEAD_DIM), jnp.float32)
    query_field = jax.random.truncated_normal(k_query, -6.0, 6.0, (TOKENS, HEADS * HEAD_DIM), jnp.float32)
    return (query_field, key_field)


def draw_queries(key, part):
    return joint_fields(key)[0].astype(jnp.bfloat16)


def draw_keys(key, part):
    return joint_fields(key)[1].astype(jnp.bfloat16)


def draw_chosen(key, part):
    count = TOKENS // BLOCK
    raw_scores = jax.random.randint(jax.random.fold_in(key, 23), (count, GROUPS, count), 0, 65536, dtype=jnp.int32)
    column = jnp.arange(count, dtype=jnp.int32)[None, None, :]
    own_block = jnp.arange(count, dtype=jnp.int32)[:, None, None]
    ranking = raw_scores * count + column
    ranking = ranking + jnp.where(column <= own_block, 2 ** 27, 0)
    ranking = ranking + jnp.where((column == 0) | (column == own_block), 2 ** 28, 0)
    ignored, picked = lax.top_k(ranking, TOPK)
    return picked.astype(jnp.int32)


def steps_of(key, dims, cuts, least, high):
    def one(dim, shards_of):
        steps = jax.random.uniform(jax.random.fold_in(jax.random.fold_in(key, 6), dim), (shards_of,), jnp.float32, least / len(cuts), high / len(cuts))
        return jnp.repeat(jnp.exp(steps), dims[dim] // shards_of).reshape((-1,) + (1,) * (len(dims) - dim - 1))

    gain = one(*cuts[0])
    for cut in cuts[1:]:
        gain = gain * one(*cut)
    return gain


def normal_values(stream_key, dims, spread, most, pieces=(), held_as=jnp.bfloat16):
    loudness = steps_of(stream_key, dims, pieces, -0.22, 0.18) if pieces else 1.0
    drawn = jax.random.normal(stream_key, dims, jnp.float32) * spread * loudness
    return jnp.minimum(jnp.maximum(drawn, -most), most).astype(held_as)


def setup_inputs(seed: int = 0) -> dict:
    streams_of = jax.random.split(jax.random.key(seed), 9)
    queries = draw_queries(jax.random.fold_in(streams_of[8], 71), 0)
    keys = draw_keys(jax.random.fold_in(streams_of[8], 71), 0)
    values = normal_values(streams_of[2], (TOKENS, GROUPS * HEAD_DIM), 1.0, 6.0, ((0, 16), (1, 8)))
    grad_out = normal_values(streams_of[3], (TOKENS, HEADS * HEAD_DIM), 1.0, 6.0, ((0, 16), (1, 8)))
    chosen = draw_chosen(jax.random.fold_in(streams_of[8], 71), 0)
    w_query = normal_values(streams_of[5], (D, HEADS * HEAD_DIM), D ** -0.5, 0.09375, ((1, 8),))
    w_key = normal_values(streams_of[6], (D, GROUPS * HEAD_DIM), D ** -0.5, 0.09375, ((1, 8),))
    w_value = normal_values(streams_of[7], (D, GROUPS * HEAD_DIM), D ** -0.5, 0.09375, ((1, 8),))
    return dict(queries=queries, keys=keys, values=values, grad_out=grad_out, chosen=chosen, w_query=w_query, w_key=w_key, w_value=w_value)


def block_grads(key_blocks, value_blocks, query_block, grad_block, picked, first_row):
    block_len = query_block.shape[0]
    head_dim = key_blocks.shape[2]
    heads_per = query_block.shape[1] // head_dim
    scaling = 1.0 / math.sqrt(head_dim)
    key_rows = (picked[:, None] * block_len + jnp.arange(block_len, dtype=jnp.int32)[None, :]).reshape(-1).astype(jnp.int32)
    chosen_keys = jnp.take(key_blocks, picked, axis=0).reshape(-1, head_dim)
    chosen_values = jnp.take(value_blocks, picked, axis=0).reshape(-1, head_dim)
    query_rows = query_block.reshape(block_len * heads_per, head_dim)
    grad_rows = grad_block.reshape(block_len * heads_per, head_dim)
    positions = first_row + jnp.repeat(jnp.arange(block_len, dtype=jnp.int32), heads_per)
    allowed = key_rows[None, :] <= positions[:, None]
    contract = (((1,), (1,)), ((), ()))
    across = (((0,), (0,)), ((), ()))
    scores = scaling * lax.dot_general(query_rows, chosen_keys, contract, preferred_element_type=jnp.float32)
    scores = jnp.where(allowed, scores, -1e+30)
    row_max = lax.optimization_barrier(jnp.max(scores, axis=1, keepdims=True))
    weights = jnp.where(allowed, jnp.exp(scores - row_max), 0.0)
    weights = weights / lax.optimization_barrier(jnp.sum(weights, axis=1, keepdims=True))
    weights_low = weights.astype(jnp.bfloat16)
    attended = jnp.dot(weights_low, chosen_values, preferred_element_type=jnp.float32)
    deltas = lax.optimization_barrier(jnp.sum(grad_rows.astype(jnp.float32) * attended, axis=1, keepdims=True))
    grad_weights = lax.dot_general(grad_rows, chosen_values, contract, preferred_element_type=jnp.float32)
    grad_scores = (weights * (grad_weights - deltas)).astype(jnp.bfloat16)
    grad_query = scaling * jnp.dot(grad_scores, chosen_keys, preferred_element_type=jnp.float32)
    grad_key = scaling * lax.dot_general(grad_scores, query_rows, across, preferred_element_type=jnp.float32)
    grad_value = lax.dot_general(weights_low, grad_rows, across, preferred_element_type=jnp.float32)
    grad_query = grad_query.astype(jnp.bfloat16).reshape(block_len, heads_per * head_dim)
    grad_key = grad_key.reshape(picked.shape[0], block_len * head_dim)
    grad_value = grad_value.reshape(picked.shape[0], block_len * head_dim)
    return (grad_query, grad_key, grad_value)

def reference(queries, keys, values, grad_out, chosen, w_query, w_key, w_value):
    heads_per = HEADS // GROUPS
    query_width = heads_per * HEAD_DIM
    blocks_here = TOK_DEV // BLOCK
    block_step = math.gcd(blocks_here, max(1, 512 // (BLOCK * heads_per)))
    turns = blocks_here // block_step
    mapped = jax.vmap(block_grads, in_axes=(None, None, 0, 0, 0, 0))

    def one_group(group_index):
        key_all = lax.dynamic_slice_in_dim(keys, (group_index * HEAD_DIM).astype(jnp.int32), HEAD_DIM, 1).reshape(NBLK, BLOCK, HEAD_DIM)
        value_all = lax.dynamic_slice_in_dim(values, (group_index * HEAD_DIM).astype(jnp.int32), HEAD_DIM, 1).reshape(NBLK, BLOCK, HEAD_DIM)
        query_part = lax.dynamic_slice_in_dim(queries, (group_index * query_width).astype(jnp.int32), query_width, 1)
        grad_part = lax.dynamic_slice_in_dim(grad_out, (group_index * query_width).astype(jnp.int32), query_width, 1)
        picked_all = lax.dynamic_index_in_dim(chosen, group_index, 1, keepdims=False)

        def one_shard(totals, shard_index):

            def update_step(running, turn_index):
                first_block = (shard_index * blocks_here + turn_index * block_step).astype(jnp.int32)
                query_set = lax.dynamic_slice_in_dim(query_part, first_block * BLOCK, block_step * BLOCK, 0).reshape(block_step, BLOCK, query_width)
                grad_set = lax.dynamic_slice_in_dim(grad_part, first_block * BLOCK, block_step * BLOCK, 0).reshape(block_step, BLOCK, query_width)
                picked_set = lax.dynamic_slice_in_dim(picked_all, first_block, block_step, 0)
                row_set = ((first_block + jnp.arange(block_step, dtype=jnp.int32)) * BLOCK).astype(jnp.int32)
                grad_q, grad_k, grad_v = mapped(key_all, value_all, query_set, grad_set, picked_set, row_set)
                flat_blocks = picked_set.reshape(-1)
                total_k = running[0].at[flat_blocks].add(grad_k.reshape(-1, BLOCK * HEAD_DIM))
                total_v = running[1].at[flat_blocks].add(grad_v.reshape(-1, BLOCK * HEAD_DIM))
                return ((total_k, total_v), grad_q.reshape(block_step * BLOCK, query_width))
            zeros_acc = jnp.zeros((NBLK, BLOCK * HEAD_DIM), jnp.float32)
            (shard_k, shard_v), grad_q = lax.scan(update_step, (zeros_acc, zeros_acc), jnp.arange(turns, dtype=jnp.int32))
            rounded_k = lax.optimization_barrier(shard_k.astype(jnp.bfloat16)).astype(jnp.float32)
            rounded_v = lax.optimization_barrier(shard_v.astype(jnp.bfloat16)).astype(jnp.float32)
            return ((totals[0] + rounded_k, totals[1] + rounded_v), grad_q.reshape(TOK_DEV, query_width))
        zeros_sum = jnp.zeros((NBLK, BLOCK * HEAD_DIM), jnp.float32)
        (total_k, total_v), grad_q = lax.scan(one_shard, (zeros_sum, zeros_sum), jnp.arange(N_CTX, dtype=jnp.int32))
        return (grad_q.reshape(TOKENS, query_width), total_k.reshape(TOKENS, HEAD_DIM).astype(jnp.bfloat16), total_v.reshape(TOKENS, HEAD_DIM).astype(jnp.bfloat16))
    grad_q_all, grad_k_all, grad_v_all = lax.map(one_group, jnp.arange(GROUPS, dtype=jnp.int32))
    grad_queries = jnp.transpose(grad_q_all, (1, 0, 2)).reshape(TOKENS, HEADS * HEAD_DIM)
    grad_keys = jnp.transpose(grad_k_all, (1, 0, 2)).reshape(TOKENS, GROUPS * HEAD_DIM)
    grad_values = jnp.transpose(grad_v_all, (1, 0, 2)).reshape(TOKENS, GROUPS * HEAD_DIM)
    contract = (((1,), (1,)), ((), ()))
    heads_shard = HEADS // N_HEAD * HEAD_DIM
    groups_shard = GROUPS // N_HEAD * HEAD_DIM
    total_input = jnp.zeros((TOKENS, D), jnp.float32)
    for shard_index in range(N_HEAD):
        query_cols = slice(shard_index * heads_shard, (shard_index + 1) * heads_shard)
        group_cols = slice(shard_index * groups_shard, (shard_index + 1) * groups_shard)
        partial_term = lax.dot_general(grad_queries[:, query_cols], w_query[:, query_cols], contract, preferred_element_type=jnp.float32)
        partial_term = partial_term + lax.dot_general(grad_keys[:, group_cols], w_key[:, group_cols], contract, preferred_element_type=jnp.float32)
        partial_term = partial_term + lax.dot_general(grad_values[:, group_cols], w_value[:, group_cols], contract, preferred_element_type=jnp.float32)
        total_input = total_input + lax.optimization_barrier(partial_term.astype(jnp.bfloat16)).astype(jnp.float32)
    return (grad_queries, grad_keys, grad_values, total_input.astype(jnp.bfloat16))
```

```python
import functools
import math

import jax
import jax.numpy as jnp
from jax import lax
from jax.experimental import pallas as pl
from jax.experimental.pallas import tpu as pltpu
from jax.sharding import PartitionSpec as P

HD = 128
BLOCK = 64
TOPK = 16
NX = 4
ROWS = 256
CHUNK = 4
OUT_W = 576
HALF_W = OUT_W // 2
SCALE = 1.0 / math.sqrt(HD)
NT = (((1,), (1,)), ((), ()))
TN = (((0,), (0,)), ((), ()))
F32 = jnp.float32
BF16 = jnp.bfloat16
N_COPIES = 128


def kernel(
    q_ref, go_ref, k_hbm, v_hbm, ch_ref, inv_ref, wq_hbm, wk_hbm, wv_hbm,
    gq_ref, gk_ref, gv_ref, gi_ref,
    kv00, kv01, kv10, kv11, gs_ref, wt_ref, qb_ref, gb_ref,
    t_ref, p_ref, s_ref, r2_ref, rl_ref, rr_ref, ys_ref, yr_ref,
    wq_ref, wk_ref, wv_ref, acc_ref, pt_ref, yb_ref, zs_ref, z2_ref, zl_ref, zr_ref, zys_ref, zyr_ref,
    send_sem, recv_sem, local_sem,
):
    c = lax.axis_index("ctx")
    h = lax.axis_index("head")
    yh, x, k = c // 8, (c // 2) % 4, c % 2
    z, yl = h // 2, h % 2
    kv_bufs = ((kv00, kv01), (kv10, kv11))

    def ctx_at(p, xx, kk):
        return p * 8 + xx * 2 + kk

    xr, xl, xo = (x + 1) % 4, (x + 3) % 4, (x + 2) % 4
    zr, zl, zo = (z + 1) % 4, (z + 3) % 4, (z + 2) % 4
    py = 1 - yh
    to_right = (ctx_at(yh, xr, k), h)
    to_left = (ctx_at(yh, xl, k), h)
    to_y = (ctx_at(py, x, k), h)
    to_core = (ctx_at(yh, x, 1 - k), h)
    to_zr = (c, zr * 2 + yl)
    to_zl = (c, zl * 2 + yl)
    to_yl = (c, z * 2 + (1 - yl))

    started = []

    def send(src, dst, where):
        i = len(started)
        copy = pltpu.make_async_remote_copy(
            src_ref=src,
            dst_ref=dst,
            send_sem=send_sem.at[i],
            recv_sem=recv_sem.at[i],
            device_id=where,
            device_id_type=pl.DeviceIdType.MESH,
        )
        copy.start()
        started.append(copy)
        return copy

    own_copies = []
    n_local = 0
    for g in range(2):
        for kv in range(2):
            src = (k_hbm, v_hbm)[kv]
            group = []
            for b in range(CHUNK):
                copy = pltpu.make_async_copy(
                    src.at[pl.ds(b * BLOCK, BLOCK), pl.ds(g * HD, HD)],
                    kv_bufs[g][kv].at[c * CHUNK + b],
                    local_sem.at[n_local],
                )
                n_local += 1
                copy.start()
                group.append(copy)
            own_copies.append(group)
    weight_copies = []
    for src, dst in ((wq_hbm, wq_ref), (wk_hbm, wk_ref), (wv_hbm, wv_ref)):
        copy = pltpu.make_async_copy(src, dst, local_sem.at[n_local])
        n_local += 1
        copy.start()
        weight_copies.append(copy)

    barrier = pltpu.get_barrier_semaphore()
    partners = (to_right, to_left, to_y, to_core, to_zr, to_zl, to_yl)
    for where in partners:
        pl.semaphore_signal(barrier, inc=1, device_id=where, device_id_type=pl.DeviceIdType.MESH)
    pl.semaphore_wait(barrier, len(partners))

    units = [(g, kv) for g in range(2) for kv in range(2)]

    def slot(u, idx):
        g, kv = units[u]
        return kv_bufs[g][kv].at[pl.ds(pl.multiple_of(idx * CHUNK, CHUNK), CHUNK)]

    def put(u, idx, where):
        return send(slot(u, idx), slot(u, idx), where)

    near, from_y, forwarded, gather_core = {}, {}, {}, []
    for u in range(4):
        for copy in own_copies[u]:
            copy.wait()
        near[u] = (put(u, c, to_right), put(u, c, to_left))
        from_y[u] = put(u, c, to_y)
        gather_core.append(put(u, c, to_core))

    def relay_plane(u, plane, arrivals):
        a_right, a_left = arrivals
        a_right.wait_recv()
        if units[u][1] == 0:
            far = put(u, ctx_at(plane, xl, k), to_right)
        gather_core.append(put(u, ctx_at(plane, xl, k), to_core))
        a_left.wait_recv()
        if units[u][1] == 1:
            far = put(u, ctx_at(plane, xr, k), to_left)
        gather_core.append(put(u, ctx_at(plane, xr, k), to_core))
        return far

    def relay_far(u, plane, far):
        far.wait_recv()
        gather_core.append(put(u, ctx_at(plane, xo, k), to_core))

    far0, near1, far1 = {}, {}, {}
    for u in range(4):
        far0[u] = relay_plane(u, yh, near[u])
        from_y[u].wait_recv()
        yi = ctx_at(py, x, k)
        near1[u] = (put(u, yi, to_right), put(u, yi, to_left))
        gather_core.append(put(u, yi, to_core))
    for u in range(4):
        relay_far(u, yh, far0[u])
    for u in range(4):
        far1[u] = relay_plane(u, py, near1[u])
    for u in range(4):
        relay_far(u, py, far1[u])
    for copy in gather_core:
        copy.wait_recv()

    base = lax.broadcasted_iota(jnp.int32, (BLOCK, HD), 0) - (
        lax.broadcasted_iota(jnp.int32, (BLOCK, HD), 1) % BLOCK
    )

    def attend(g, q):
        own = c * CHUNK + q
        rows = pl.ds(pl.multiple_of(q * BLOCK, BLOCK), BLOCK)
        qb = jnp.concatenate([q_ref[rows, pl.ds((2 * g + i) * HD, HD)] for i in range(2)], axis=0)
        gb = jnp.concatenate([go_ref[rows, pl.ds((2 * g + i) * HD, HD)] for i in range(2)], axis=0)
        qb_ref[g, q] = qb
        gb_ref[g, q] = gb
        blocks = [ch_ref[q * 32 + g * TOPK + s] for s in range(TOPK)]
        kc = jnp.concatenate([kv_bufs[g][0][b] for b in blocks], axis=0)
        scores = SCALE * lax.dot_general(kc, qb, NT, preferred_element_type=F32)
        scores = jnp.concatenate(
            [
                jnp.where(
                    base <= (own - blocks[s]) * BLOCK,
                    scores[s * BLOCK : (s + 1) * BLOCK],
                    -1e30,
                )
                for s in range(TOPK)
            ],
            axis=0,
        )
        top = jnp.max(scores, axis=0, keepdims=True)
        weights = jnp.exp(scores - top)
        weights = weights * (1.0 / jnp.sum(weights, axis=0, keepdims=True))
        low = weights.astype(BF16)
        vc = jnp.concatenate([kv_bufs[g][1][b] for b in blocks], axis=0)
        grad_w = lax.dot_general(vc, gb, NT, preferred_element_type=F32)
        deltas = jnp.sum(low.astype(F32) * grad_w, axis=0, keepdims=True)
        grad_s = (weights * (grad_w - deltas)).astype(BF16)
        grad_q = SCALE * lax.dot_general(grad_s, kc, TN, preferred_element_type=F32)
        for i in range(2):
            gq_ref[rows, pl.ds((2 * g + i) * HD, HD)] = grad_q[i * BLOCK : (i + 1) * BLOCK].astype(BF16)
        for s in range(TOPK):
            gs_ref[g, q, s] = grad_s[s * BLOCK : (s + 1) * BLOCK]
            wt_ref[g, q, s] = low[s * BLOCK : (s + 1) * BLOCK]

    def terms(g):
        for q in range(CHUNK):
            gs_ref[g, q, TOPK] = jnp.zeros((BLOCK, HD), BF16)
            wt_ref[g, q, TOPK] = jnp.zeros((BLOCK, HD), BF16)

        def body(i, carry):
            for kv, (src, rhs) in enumerate(((gs_ref, qb_ref), (wt_ref, gb_ref))):
                right = jnp.concatenate([rhs[g, q] for q in range(CHUNK)], axis=0)
                lines = []
                for b in range(2 * CHUNK):
                    j = i * (2 * CHUNK) + b
                    lines.append(
                        jnp.concatenate(
                            [src[g, q, inv_ref[g * 256 + q * 64 + j]] for q in range(CHUNK)], axis=1
                        )
                    )
                out = jnp.dot(jnp.concatenate(lines, axis=0), right, preferred_element_type=F32)
                if kv == 0:
                    out = SCALE * out
                out = out.astype(BF16)
                t_ref[2 * g + kv, 0, i] = out[:ROWS]
                t_ref[2 * g + kv, 1, i] = out[ROWS:]
            return carry

        lax.fori_loop(0, 8, body, 0)

    core_sums = {}
    for g in range(2):
        def step(q, carry, g=g):
            attend(g, q)
            return carry

        lax.fori_loop(0, CHUNK, step, 0)
        terms(g)
        for kv in range(2):
            u = 2 * g + kv
            core_sums[u] = send(t_ref.at[u, 1 - k], p_ref.at[u], to_core)

    def ring_start(way, mine, r2, rl, rr, places, ends):
        here, right, left, across = places
        go_right, go_left = ends
        if way == 0:
            far = send(mine.at[across], r2, go_right)
            direct = send(mine.at[left], rr, go_left)
        else:
            far = send(mine.at[across], r2, go_left)
            direct = send(mine.at[right], rl, go_right)
        return far, direct

    def ring_relay(way, mine, r2, rl, rr, places, ends, flying):
        here, right, left, across = places
        go_right, go_left = ends
        far, direct = flying
        far.wait_recv()
        i = right if way == 0 else left
        mine[i] = (mine[i].astype(F32) + r2[...].astype(F32)).astype(BF16)
        last = send(mine.at[i], rl if way == 0 else rr, go_right if way == 0 else go_left)
        return last, direct

    def ring_end(mine, rl, rr, places, flying):
        for copy in flying:
            copy.wait_recv()
        return mine[places[0]].astype(F32) + rl[...].astype(F32) + rr[...].astype(F32)

    x_places, x_ends = (x, xr, xl, xo), (to_right, to_left)
    z_places, z_ends = (z, zr, zl, zo), (to_zr, to_zl)

    def x_args(u, plane, n):
        return s_ref.at[u, plane], r2_ref.at[u, n], rl_ref.at[u, n], rr_ref.at[u, n], x_places, x_ends

    flying = {}
    for u in range(4):
        core_sums[u].wait_recv()
        for plane in range(2):
            for xx in range(4):
                i = plane * 4 + xx
                s_ref[u, plane, xx] = (
                    t_ref[u, k, i].astype(F32) + p_ref[u, i].astype(F32)
                ).astype(BF16)
        flying[u, 0] = ring_start(u % 2, *x_args(u, py, 0))
    for u in range(4):
        flying[u, 1] = ring_start(u % 2, *x_args(u, yh, 1))

    for copy in weight_copies:
        copy.wait()

    def query_part(i, carry):
        rows = pl.ds(pl.multiple_of(i * OUT_W, OUT_W), OUT_W)
        acc_ref[rows, :] = lax.dot_general(wq_ref[rows, :], gq_ref[...], NT, preferred_element_type=F32)
        return carry

    lax.fori_loop(0, 8, query_part, 0)

    for u in range(4):
        flying[u, 0] = ring_relay(u % 2, *x_args(u, py, 0), flying[u, 0])
    from_plane = {}
    for u in range(4):
        flying[u, 1] = ring_relay(u % 2, *x_args(u, yh, 1), flying[u, 1])
    for u in range(4):
        mine, _, rl, rr, places, _ = x_args(u, py, 0)
        ys_ref[u] = ring_end(mine, rl, rr, places, flying[u, 0]).astype(BF16)
        from_plane[u] = send(ys_ref.at[u], yr_ref.at[u], to_y)
    for u in range(4):
        g, kv = units[u]
        mine, _, rl, rr, places, _ = x_args(u, yh, 1)
        total = ring_end(mine, rl, rr, places, flying[u, 1])
        from_plane[u].wait_recv()
        total = total + yr_ref[u].astype(F32)
        (gk_ref, gv_ref)[kv][:, pl.ds(g * HD, HD)] = total.astype(BF16)

    def key_value_part(i, carry):
        rows = pl.ds(pl.multiple_of(i * OUT_W, OUT_W), OUT_W)
        out = acc_ref[rows, :]
        out = out + lax.dot_general(wk_ref[rows, :], gk_ref[...], NT, preferred_element_type=F32)
        out = out + lax.dot_general(wv_ref[rows, :], gv_ref[...], NT, preferred_element_type=F32)
        out = out.astype(BF16)
        for t in range(2):
            for w in range(2):
                pt_ref[t, w, i % 2, i // 2] = out[w * HALF_W : (w + 1) * HALF_W, t * HD : (t + 1) * HD]
        return carry

    lax.fori_loop(0, 8, key_value_part, 0)

    def z_args(n, mine):
        return mine, z2_ref.at[n], zl_ref.at[n], zr_ref.at[n], z_places, z_ends

    y_first = [send(pt_ref.at[1, w, 1 - yl], yb_ref.at[w], to_yl) for w in range(2)]
    z_work = {}
    for w in range(2):
        z_work[w] = (w, z_args(w, pt_ref.at[0, w, 1 - yl]))
        z_work[2 + w] = (w, z_args(2 + w, pt_ref.at[0, w, yl]))
        z_work[4 + w] = (w, z_args(4 + w, zs_ref.at[w]))
    fly = {n: ring_start(z_work[n][0], *z_work[n][1]) for n in range(4)}
    for n in range(2):
        fly[n] = ring_relay(z_work[n][0], *z_work[n][1], fly[n])
    for w in range(2):
        y_first[w].wait_recv()
        for i in range(4):
            zs_ref[w, i] = (pt_ref[1, w, yl, i].astype(F32) + yb_ref[w, i].astype(F32)).astype(BF16)
        fly[4 + w] = ring_start(w, *z_work[4 + w][1])
    y_last = []
    for w in range(2):
        mine, _, a, b, places, _ = z_work[w][1]
        zys_ref[w] = ring_end(mine, a, b, places, fly[w]).astype(BF16)
        y_last.append(send(zys_ref.at[w], zyr_ref.at[w], to_yl))
    for n in range(2, 6):
        fly[n] = ring_relay(z_work[n][0], *z_work[n][1], fly[n])
    for w in range(2):
        mine, _, a, b, places, _ = z_work[2 + w][1]
        total = ring_end(mine, a, b, places, fly[2 + w])
        y_last[w].wait_recv()
        total = total + zyr_ref[w].astype(F32)
        gi_ref[pl.ds(w * HALF_W, HALF_W), pl.ds(0, HD)] = total.astype(BF16)
    for w in range(2):
        mine, _, a, b, places, _ = z_work[4 + w][1]
        total = ring_end(mine, a, b, places, fly[4 + w])
        gi_ref[pl.ds(w * HALF_W, HALF_W), pl.ds(HD, HD)] = total.astype(BF16)

    for copy in started:
        copy.wait_send()


def body(queries, keys, values, grad_out, chosen, w_query, w_key, w_value):
    slots = jnp.arange(TOPK, dtype=jnp.int32)[None, None, :, None]
    names = jnp.arange(64, dtype=jnp.int32)[None, None, None, :]
    inverse = jnp.min(jnp.where(chosen[..., None] == names, slots, TOPK), axis=2)
    inverse = inverse.transpose(1, 0, 2).reshape(-1)
    vmem = pl.BlockSpec(memory_space=pltpu.VMEM)
    smem = pl.BlockSpec(memory_space=pltpu.SMEM)
    hbm = pl.BlockSpec(memory_space=pl.ANY)
    shape = jax.ShapeDtypeStruct
    buf = lambda *dims: pltpu.VMEM(dims, BF16)
    chunk = (ROWS, HD)
    zc = (HALF_W, HD)
    grad_queries, grad_keys, grad_values, grad_input = pl.pallas_call(
        kernel,
        out_shape=(
            shape((ROWS, 512), BF16),
            shape((ROWS, 256), BF16),
            shape((ROWS, 256), BF16),
            shape((OUT_W, ROWS), BF16),
        ),
        in_specs=[vmem, vmem, hbm, hbm, smem, smem, hbm, hbm, hbm],
        out_specs=(vmem, vmem, vmem, vmem),
        scratch_shapes=[
            buf(64, BLOCK, HD), buf(64, BLOCK, HD), buf(64, BLOCK, HD), buf(64, BLOCK, HD),
            buf(2, CHUNK, TOPK + 1, BLOCK, HD), buf(2, CHUNK, TOPK + 1, BLOCK, HD),
            buf(2, CHUNK, HD, HD), buf(2, CHUNK, HD, HD),
            buf(4, 2, 8, *chunk), buf(4, 8, *chunk), buf(4, 2, 4, *chunk),
            buf(4, 2, *chunk), buf(4, 2, *chunk), buf(4, 2, *chunk), buf(4, *chunk), buf(4, *chunk),
            buf(4608, 512), buf(4608, 256), buf(4608, 256), pltpu.VMEM((4608, ROWS), F32),
            buf(2, 2, 2, 4, *zc), buf(2, 4, *zc), buf(2, 4, *zc),
            buf(6, *zc), buf(6, *zc), buf(6, *zc), buf(2, *zc), buf(2, *zc),
            pltpu.SemaphoreType.DMA((N_COPIES,)),
            pltpu.SemaphoreType.DMA((N_COPIES,)),
            pltpu.SemaphoreType.DMA((19,)),
        ],
        compiler_params=pltpu.CompilerParams(
            collective_id=0, has_side_effects=True, vmem_limit_bytes=60 * 1024 * 1024
        ),
    )(queries, grad_out, keys, values, chosen.reshape(-1), inverse, w_query, w_key, w_value)
    return grad_queries, grad_keys, grad_values, grad_input.T


def solution(mesh):
    both = P("ctx", "head")
    return jax.shard_map(
        body,
        mesh=mesh,
        in_specs=(both, both, both, both, P("ctx", "head", None)) + (P(None, "head"),) * 3,
        out_specs=(both, both, both, both),
        check_vma=False,
    )
```

```python
import functools
import math

import jax
import jax.numpy as jnp
from jax import lax
from jax.experimental import pallas as pl
from jax.experimental.pallas import tpu as pltpu
from jax.sharding import PartitionSpec as P

HD = 128
BLOCK = 64
TOPK = 16
NX = 4
ROWS = 256
CHUNK = 4
OUT_W = 576
HALF_W = OUT_W // 2
SCALE = 1.0 / math.sqrt(HD)
NT = (((1,), (1,)), ((), ()))
TN = (((0,), (0,)), ((), ()))
F32 = jnp.float32
BF16 = jnp.bfloat16
N_COPIES = 144


def kernel(
    q_hbm, go_hbm, k_hbm, v_hbm, ch_ref, inv_ref, wq_hbm, wk_hbm, wv_hbm,
    gq_hbm, gk_hbm, gv_hbm, gi_hbm,
    kv00, kv01, kv10, kv11, q_ref, go_ref, gq_ref, gk_ref, gv_ref, gi_ref,
    gs_ref, wt_ref, qb_ref, gb_ref,
    t_ref, p_ref, s_ref, xa_ref, xf_ref, xl_ref, xr_ref, xs_ref, xy_ref,
    wq_ref, wk_ref, wv_ref, acc_ref, pt_ref, za_ref, zf_ref, zl_ref, zr_ref, zs_ref, zy_ref,
    send_sem, recv_sem, local_sem,
):
    c = lax.axis_index("ctx")
    h = lax.axis_index("head")
    yh, x, k = c // 8, (c // 2) % 4, c % 2
    z, yl = h // 2, h % 2
    kv_bufs = ((kv00, kv01), (kv10, kv11))

    def ctx_at(p, xx, kk):
        return p * 8 + xx * 2 + kk

    xr, xl, xo = (x + 1) % 4, (x + 3) % 4, (x + 2) % 4
    zr, zl, zo = (z + 1) % 4, (z + 3) % 4, (z + 2) % 4
    py = 1 - yh
    to_right = (ctx_at(yh, xr, k), h)
    to_left = (ctx_at(yh, xl, k), h)
    to_y = (ctx_at(py, x, k), h)
    to_core = (ctx_at(yh, x, 1 - k), h)
    to_zr = (c, zr * 2 + yl)
    to_zl = (c, zl * 2 + yl)
    to_yl = (c, z * 2 + (1 - yl))

    started = []

    def plan(src, dst, where):
        i = len(started)
        copy = pltpu.make_async_remote_copy(
            src_ref=src,
            dst_ref=dst,
            send_sem=send_sem.at[i],
            recv_sem=recv_sem.at[i],
            device_id=where,
            device_id_type=pl.DeviceIdType.MESH,
        )
        started.append(copy)
        return copy

    def send(src, dst, where):
        copy = plan(src, dst, where)
        copy.start()
        return copy

    barrier = pltpu.get_barrier_semaphore()
    partners = (to_right, to_left, to_y, to_core, to_zr, to_zl, to_yl)
    for where in partners:
        pl.semaphore_signal(barrier, inc=1, device_id=where, device_id_type=pl.DeviceIdType.MESH)

    own_copies = []
    n_local = 0
    for g in range(2):
        for kv in range(2):
            src = (k_hbm, v_hbm)[kv]
            group = []
            for b in range(CHUNK):
                copy = pltpu.make_async_copy(
                    src.at[pl.ds(b * BLOCK, BLOCK), pl.ds(g * HD, HD)],
                    kv_bufs[g][kv].at[c * CHUNK + b],
                    local_sem.at[n_local],
                )
                n_local += 1
                copy.start()
                group.append(copy)
            own_copies.append(group)

    def local(src, dst):
        nonlocal n_local
        copy = pltpu.make_async_copy(src, dst, local_sem.at[n_local])
        n_local += 1
        copy.start()
        return copy

    query_copies = [local(q_hbm, q_ref), local(go_hbm, go_ref)]
    weight_copies = [local(wq_hbm, wq_ref), local(wk_hbm, wk_ref), local(wv_hbm, wv_ref)]
    out_copies = []

    pl.semaphore_wait(barrier, len(partners))

    units = [(g, kv) for g in range(2) for kv in range(2)]

    def slot(u, idx):
        g, kv = units[u]
        return kv_bufs[g][kv].at[pl.ds(pl.multiple_of(idx * CHUNK, CHUNK), CHUNK)]

    def put(u, idx, where):
        return plan(slot(u, idx), slot(u, idx), where)

    g_near, g_far, g_core, g_y = {}, {}, {}, {}
    for u in range(4):
        g_y[u] = put(u, c, to_y)
        for n, plane in enumerate((yh, py)):
            first = ctx_at(plane, x, k)
            g_near[u, n] = (put(u, first, to_right), put(u, first, to_left))
            if n == 1:
                g_far[u, n] = put(u, ctx_at(yh, xo, k), to_y)
            elif units[u][1] == 0:
                g_far[u, n] = put(u, ctx_at(plane, xl, k), to_right)
            else:
                g_far[u, n] = put(u, ctx_at(plane, xr, k), to_left)
            g_core[u, n] = [put(u, ctx_at(plane, xx, k), to_core) for xx in (x, xl, xr, xo)]

    def gather_first(u):
        for copy in own_copies[u]:
            copy.wait()
        g_near[u, 0][0].start()
        g_near[u, 0][1].start()
        g_y[u].start()
        g_core[u, 0][0].start()

    def gather_relay(u, n):
        for side in range(2):
            g_near[u, n][side].wait_recv()
            if n == 0 and units[u][1] == side:
                g_far[u, 0].start()
            g_core[u, n][1 + side].start()

    def gather_y(u):
        g_y[u].wait_recv()
        g_near[u, 1][0].start()
        g_near[u, 1][1].start()
        g_core[u, 1][0].start()

    def gather_far(u, n):
        g_far[u, n].wait_recv()
        if n == 0:
            g_far[u, 1].start()
        g_core[u, n][3].start()

    def gather_end(u):
        for n in range(2):
            for copy in g_core[u, n]:
                copy.wait_recv()

    def each(step, *names):
        for name in names:
            step(*name)

    each(gather_first, (0,), (1,))
    for u in (0, 1):
        gather_relay(u, 0)
        gather_y(u)
    each(gather_first, (2,), (3,))
    each(gather_far, (0, 0), (1, 0))
    each(gather_relay, (0, 1), (1, 1))
    for u in (2, 3):
        gather_relay(u, 0)
        gather_y(u)
    each(gather_far, (0, 1), (1, 1))
    each(gather_end, (0,), (1,))
    for copy in query_copies:
        copy.wait()

    base = lax.broadcasted_iota(jnp.int32, (BLOCK, HD), 0) - (
        lax.broadcasted_iota(jnp.int32, (BLOCK, HD), 1) % BLOCK
    )

    def attend(g, q):
        own = c * CHUNK + q
        rows = pl.ds(pl.multiple_of(q * BLOCK, BLOCK), BLOCK)
        qb = jnp.concatenate([q_ref[rows, pl.ds((2 * g + i) * HD, HD)] for i in range(2)], axis=0)
        gb = jnp.concatenate([go_ref[rows, pl.ds((2 * g + i) * HD, HD)] for i in range(2)], axis=0)
        qb_ref[g, q] = qb
        gb_ref[g, q] = gb
        blocks = [ch_ref[q, g, s] for s in range(TOPK)]
        kc = jnp.concatenate([kv_bufs[g][0][b] for b in blocks], axis=0)
        scores = SCALE * lax.dot_general(kc, qb, NT, preferred_element_type=F32)
        scores = jnp.concatenate(
            [
                jnp.where(
                    base <= (own - blocks[s]) * BLOCK,
                    scores[s * BLOCK : (s + 1) * BLOCK],
                    -1e30,
                )
                for s in range(TOPK)
            ],
            axis=0,
        )
        top = jnp.max(scores, axis=0, keepdims=True)
        weights = jnp.exp(scores - top)
        weights = weights * (1.0 / jnp.sum(weights, axis=0, keepdims=True))
        low = weights.astype(BF16)
        vc = jnp.concatenate([kv_bufs[g][1][b] for b in blocks], axis=0)
        grad_w = lax.dot_general(vc, gb, NT, preferred_element_type=F32)
        deltas = jnp.sum(low.astype(F32) * grad_w, axis=0, keepdims=True)
        grad_s = (weights * (grad_w - deltas)).astype(BF16)
        grad_q = SCALE * lax.dot_general(grad_s, kc, TN, preferred_element_type=F32)
        for i in range(2):
            gq_ref[rows, pl.ds((2 * g + i) * HD, HD)] = grad_q[i * BLOCK : (i + 1) * BLOCK].astype(BF16)
        for s in range(TOPK):
            gs_ref[g, q, s] = grad_s[s * BLOCK : (s + 1) * BLOCK]
            wt_ref[g, q, s] = low[s * BLOCK : (s + 1) * BLOCK]

    for g in range(2):
        for q in range(CHUNK):
            gs_ref[g, q, TOPK] = jnp.zeros((BLOCK, HD), BF16)
            wt_ref[g, q, TOPK] = jnp.zeros((BLOCK, HD), BF16)

    def terms(g, plane):
        def body(i, carry):
            for kv, (src, rhs) in enumerate(((gs_ref, qb_ref), (wt_ref, gb_ref))):
                right = jnp.concatenate([rhs[g, q] for q in range(CHUNK)], axis=0)
                lines = []
                for b in range(2 * CHUNK):
                    j = (plane * 4 + i) * (2 * CHUNK) + b
                    lines.append(
                        jnp.concatenate(
                            [src[g, q, inv_ref[q, g, j]] for q in range(CHUNK)], axis=1
                        )
                    )
                out = jnp.dot(jnp.concatenate(lines, axis=0), right, preferred_element_type=F32)
                if kv == 0:
                    out = SCALE * out
                out = out.astype(BF16)
                t_ref[2 * g + kv, plane, 0, i] = out[:ROWS]
                t_ref[2 * g + kv, plane, 1, i] = out[ROWS:]
            return carry

        lax.fori_loop(0, 4, body, 0)

    planes = (py, yh)
    core_sums = {
        (u, n): plan(t_ref.at[u, planes[n], 1 - k], p_ref.at[u, planes[n]], to_core)
        for u in range(4)
        for n in range(2)
    }

    class Sum:
        def __init__(self, way, theirs, mine, bufs, places, ends, over):
            self.way, self.theirs, self.mine, self.bufs = way, theirs, mine, bufs
            self.here, right, left, across = places
            self.across = across
            go_right, go_left = ends
            first, far, l0, r0, l1, r1, stage, last = bufs
            self.first = plan(theirs.at[across], first, over)
            self.theirs_right = plan(theirs.at[right], l1, go_right)
            self.theirs_left = plan(theirs.at[left], r1, go_left)
            self.far = plan(mine.at[across], far, go_right if way == 0 else go_left)
            self.mine_right = plan(mine.at[right], l0, go_right)
            self.mine_left = plan(mine.at[left], r0, go_left)
            self.relayed, self.direct = (
                (self.mine_right, self.mine_left) if way == 0 else (self.mine_left, self.mine_right)
            )
            self.relay_at = right if way == 0 else left
            self.over = plan(stage, last, over)

        def start_theirs(self):
            self.first.start()
            self.theirs_right.start()
            self.theirs_left.start()

        def start_mine(self):
            self.direct.start()

        def add(self, i, buf):
            self.mine[i] = (self.mine[i].astype(F32) + buf[...].astype(F32)).astype(BF16)

        def go_far(self):
            self.first.wait_recv()
            self.add(self.across, self.bufs[0])
            self.far.start()

        def cross(self):
            _, _, _, _, l1, r1, stage, _ = self.bufs
            self.theirs_right.wait_recv()
            self.theirs_left.wait_recv()
            total = self.theirs[self.here].astype(F32) + l1[...].astype(F32) + r1[...].astype(F32)
            stage[...] = total.astype(BF16)
            self.over.start()

        def relay(self):
            self.far.wait_recv()
            self.add(self.relay_at, self.bufs[1])
            self.relayed.start()

        def end(self):
            _, _, l0, r0, _, _, _, last = self.bufs
            self.mine_right.wait_recv()
            self.mine_left.wait_recv()
            total = self.mine[self.here].astype(F32) + l0[...].astype(F32) + r0[...].astype(F32)
            self.over.wait_recv()
            return total + last[...].astype(F32)

    x_sums = [
        Sum(
            u % 2, s_ref.at[u, py], s_ref.at[u, yh],
            (xa_ref.at[u], xf_ref.at[u], xl_ref.at[u, 0], xr_ref.at[u, 0],
             xl_ref.at[u, 1], xr_ref.at[u, 1], xs_ref.at[u], xy_ref.at[u]),
            (x, xr, xl, xo), (to_right, to_left), to_y,
        )
        for u in range(4)
    ]

    def core_sum(u, n):
        plane = planes[n]
        core_sums[u, n].wait_recv()
        for xx in range(4):
            s_ref[u, plane, xx] = (
                t_ref[u, plane, k, xx].astype(F32) + p_ref[u, plane, xx].astype(F32)
            ).astype(BF16)
        if n == 0:
            x_sums[u].start_theirs()
        else:
            x_sums[u].start_mine()

    def sum_end(u):
        g, kv = units[u]
        (gk_ref, gv_ref)[kv][:, pl.ds(g * HD, HD)] = x_sums[u].end().astype(BF16)

    def do(names, *steps):
        for step in steps:
            for u in names:
                getattr(x_sums[u], step)()

    def core_start(g, n):
        core_sums[2 * g, n].start()
        core_sums[2 * g + 1, n].start()

    hooks = {
        (0, 1): lambda: (each(gather_far, (2, 0), (3, 0)), each(gather_relay, (2, 1), (3, 1))),
        (0, 3): lambda: each(gather_far, (2, 1), (3, 1)),
        (1, 1): lambda: each(core_sum, (0, 0), (1, 0), (0, 1), (1, 1)),
        (1, 3): lambda: do((0, 1), "go_far", "cross"),
    }
    for g in range(2):
        if g == 1:
            each(gather_end, (2,), (3,))

        def step(q, carry, g=g):
            for (gg, at), action in hooks.items():
                if gg == g:
                    pl.when(q == at)(lambda action=action: (action(), None)[1])
            attend(g, q)
            return carry

        lax.fori_loop(0, CHUNK, step, 0)
        if g == 1:
            out_copies.append(local(gq_ref, gq_hbm))
        for n in range(2):
            terms(g, planes[n])
            core_start(g, n)
            if g == 1 and n == 0:
                do((0, 1), "relay")
    each(core_sum, (2, 0), (3, 0))

    for copy in weight_copies:
        copy.wait()

    def query_part(i, carry):
        rows = pl.ds(pl.multiple_of(i * OUT_W, OUT_W), OUT_W)
        acc_ref[rows, :] = lax.dot_general(wq_ref[rows, :], gq_ref[...], NT, preferred_element_type=F32)
        return carry

    lax.fori_loop(0, 3, query_part, 0)
    each(core_sum, (2, 1), (3, 1))
    lax.fori_loop(3, 6, query_part, 0)
    do((2, 3), "go_far")
    do((2, 3), "cross")
    lax.fori_loop(6, 8, query_part, 0)
    do((2, 3), "relay")
    each(sum_end, (0,), (1,), (2,), (3,))
    out_copies.append(local(gk_ref, gk_hbm))
    out_copies.append(local(gv_ref, gv_hbm))

    z_places = (z, zr, zl, zo)
    z_sums = [
        Sum(
            w, pt_ref.at[w, 1 - yl], pt_ref.at[w, yl],
            (za_ref.at[w], zf_ref.at[w], zl_ref.at[w, 0], zr_ref.at[w, 0],
             zl_ref.at[w, 1], zr_ref.at[w, 1], zs_ref.at[w], zy_ref.at[w]),
            z_places, (to_zr, to_zl), to_yl,
        )
        for w in range(2)
    ]

    def term_chunk(side, zz):
        i = zz * 2 + side
        rows = pl.ds(pl.multiple_of(i * OUT_W, OUT_W), OUT_W)
        out = acc_ref[rows, :]
        out = out + lax.dot_general(wk_ref[rows, :], gk_ref[...], NT, preferred_element_type=F32)
        out = out + lax.dot_general(wv_ref[rows, :], gv_ref[...], NT, preferred_element_type=F32)
        out = out.astype(BF16)
        for w in range(2):
            pt_ref[w, side, zz] = out[w * HALF_W : (w + 1) * HALF_W]

    def both(step):
        for w in range(2):
            step(z_sums[w])

    term_chunk(1 - yl, zo)
    both(lambda t: t.first.start())
    term_chunk(1 - yl, zr)
    both(lambda t: t.theirs_right.start())
    term_chunk(1 - yl, zl)
    both(lambda t: t.theirs_left.start())
    term_chunk(yl, zl)
    z_sums[0].direct.start()
    term_chunk(yl, zr)
    z_sums[1].direct.start()
    term_chunk(yl, zo)
    both(lambda t: t.go_far())
    term_chunk(1 - yl, z)
    term_chunk(yl, z)
    both(lambda t: t.cross())
    both(lambda t: t.relay())
    for w in range(2):
        gi_ref[pl.ds(w * HALF_W, HALF_W), :] = z_sums[w].end().astype(BF16)
        out_copies.append(
            local(gi_ref.at[pl.ds(w * HALF_W, HALF_W)], gi_hbm.at[pl.ds(w * HALF_W, HALF_W)])
        )

    for copy in out_copies:
        copy.wait()
    for copy in started:
        copy.wait_send()


def write_out(*refs):
    for src, dst in zip(refs[:4], refs[4:]):
        dst[...] = src[...]


def body(queries, keys, values, grad_out, chosen, w_query, w_key, w_value):
    slots = jnp.arange(TOPK, dtype=jnp.int32)[None, None, :, None]
    names = jnp.arange(64, dtype=jnp.int32)[None, None, None, :]
    inverse = jnp.min(jnp.where(chosen[..., None] == names, slots, TOPK), axis=2)
    vmem = pl.BlockSpec(memory_space=pltpu.VMEM)
    smem = pl.BlockSpec(memory_space=pltpu.SMEM)
    hbm = pl.BlockSpec(memory_space=pl.ANY)
    shape = jax.ShapeDtypeStruct
    buf = lambda *dims: pltpu.VMEM(dims, BF16)
    chunk = (ROWS, HD)
    zc = (HALF_W, ROWS)
    outs = pl.pallas_call(
        kernel,
        out_shape=(
            shape((ROWS, 512), BF16),
            shape((ROWS, 256), BF16),
            shape((ROWS, 256), BF16),
            shape((OUT_W, ROWS), BF16),
        ),
        in_specs=[hbm, hbm, hbm, hbm, smem, smem, hbm, hbm, hbm],
        out_specs=(hbm,) * 4,
        scratch_shapes=[
            buf(64, BLOCK, HD), buf(64, BLOCK, HD), buf(64, BLOCK, HD), buf(64, BLOCK, HD),
            buf(ROWS, 512), buf(ROWS, 512), buf(ROWS, 512), buf(ROWS, 256), buf(ROWS, 256), buf(OUT_W, ROWS),
            buf(2, CHUNK, TOPK + 1, BLOCK, HD), buf(2, CHUNK, TOPK + 1, BLOCK, HD),
            buf(2, CHUNK, HD, HD), buf(2, CHUNK, HD, HD),
            buf(4, 2, 2, 4, *chunk), buf(4, 2, 4, *chunk), buf(4, 2, 4, *chunk),
            buf(4, *chunk), buf(4, *chunk), buf(4, 2, *chunk), buf(4, 2, *chunk), buf(4, *chunk), buf(4, *chunk),
            buf(4608, 512), buf(4608, 256), buf(4608, 256), pltpu.VMEM((4608, ROWS), F32),
            buf(2, 2, 4, *zc), buf(2, *zc), buf(2, *zc),
            buf(2, 2, *zc), buf(2, 2, *zc), buf(2, *zc), buf(2, *zc),
            pltpu.SemaphoreType.DMA((N_COPIES,)),
            pltpu.SemaphoreType.DMA((N_COPIES,)),
            pltpu.SemaphoreType.DMA((32,)),
        ],
        compiler_params=pltpu.CompilerParams(
            collective_id=0, has_side_effects=True, vmem_limit_bytes=60 * 1024 * 1024
        ),
    )(queries, grad_out, keys, values, chosen, inverse, w_query, w_key, w_value)
    grad_queries, grad_keys, grad_values, grad_input = pl.pallas_call(
        write_out,
        out_shape=tuple(shape(o.shape, o.dtype) for o in outs),
        in_specs=[vmem] * 4,
        out_specs=(vmem,) * 4,
    )(*outs)
    return grad_queries, grad_keys, grad_values, grad_input.T


def solution(mesh):
    both = P("ctx", "head")
    return jax.shard_map(
        body,
        mesh=mesh,
        in_specs=(both, both, both, both, P("ctx", "head", None)) + (P(None, "head"),) * 3,
        out_specs=(both, both, both, both),
        check_vma=False,
    )
```

```python
import functools
import math

import jax
import jax.numpy as jnp
from jax import lax
from jax.experimental import pallas as pl
from jax.experimental.pallas import tpu as pltpu
from jax.sharding import PartitionSpec as P

HD = 128
BLOCK = 64
TOPK = 16
NX = 4
ROWS = 256
CHUNK = 4
OUT_W = 576
HALF_W = OUT_W // 2
HALF_K = TOPK * BLOCK // 2
SCALE = 1.0 / math.sqrt(HD)
EXP2_SCALE = SCALE / math.log(2.0)
NT = (((1,), (1,)), ((), ()))
TN = (((0,), (0,)), ((), ()))
F32 = jnp.float32
BF16 = jnp.bfloat16
N_COPIES = 144


def kernel(
    q_hbm, go_hbm, k_hbm, v_hbm, ch_ref, chv_ref, wq_hbm, wk_hbm, wv_hbm,
    gq_hbm, gk_hbm, gv_hbm, gi_hbm,
    kv00, kv01, kv10, kv11, q_ref, go_ref, gq_ref, gk_ref, gv_ref, gi_ref,
    tm_ref, names_ref, inv_ref,
    t_ref, p_ref, s_ref, xa_ref, xf_ref, xl_ref, xr_ref, xs_ref, xy_ref,
    wq_ref, wk_ref, wv_ref, acc_ref, pt_ref, za_ref, zf_ref, zl_ref, zr_ref, zs_ref, zy_ref,
    send_sem, recv_sem, local_sem,
):
    c = lax.axis_index("ctx")
    h = lax.axis_index("head")
    yh, x, k = c // 8, (c // 2) % 4, c % 2
    z, yl = h // 2, h % 2
    kv_bufs = ((kv00, kv01), (kv10, kv11))

    def ctx_at(p, xx, kk):
        return p * 8 + xx * 2 + kk

    xr, xl, xo = (x + 1) % 4, (x + 3) % 4, (x + 2) % 4
    zr, zl, zo = (z + 1) % 4, (z + 3) % 4, (z + 2) % 4
    py = 1 - yh
    to_right = (ctx_at(yh, xr, k), h)
    to_left = (ctx_at(yh, xl, k), h)
    to_y = (ctx_at(py, x, k), h)
    to_core = (ctx_at(yh, x, 1 - k), h)
    to_zr = (c, zr * 2 + yl)
    to_zl = (c, zl * 2 + yl)
    to_yl = (c, z * 2 + (1 - yl))

    started = []

    def plan(src, dst, where):
        i = len(started)
        copy = pltpu.make_async_remote_copy(
            src_ref=src,
            dst_ref=dst,
            send_sem=send_sem.at[i],
            recv_sem=recv_sem.at[i],
            device_id=where,
            device_id_type=pl.DeviceIdType.MESH,
        )
        started.append(copy)
        return copy

    def send(src, dst, where):
        copy = plan(src, dst, where)
        copy.start()
        return copy

    barrier = pltpu.get_barrier_semaphore()
    partners = (to_right, to_left, to_y, to_core, to_zr, to_zl, to_yl)
    for where in partners:
        pl.semaphore_signal(barrier, inc=1, device_id=where, device_id_type=pl.DeviceIdType.MESH)

    own_copies = []
    n_local = 0
    for g in range(2):
        for kv in range(2):
            src = (k_hbm, v_hbm)[kv]
            group = []
            for b in range(CHUNK):
                copy = pltpu.make_async_copy(
                    src.at[pl.ds(b * BLOCK, BLOCK), pl.ds(g * HD, HD)],
                    kv_bufs[g][kv].at[c * CHUNK + b],
                    local_sem.at[n_local],
                )
                n_local += 1
                copy.start()
                group.append(copy)
            own_copies.append(group)

    def local(src, dst):
        nonlocal n_local
        copy = pltpu.make_async_copy(src, dst, local_sem.at[n_local])
        n_local += 1
        copy.start()
        return copy

    query_copies = [local(q_hbm, q_ref), local(go_hbm, go_ref)]
    weight_copies = [local(wq_hbm, wq_ref), local(wk_hbm, wk_ref), local(wv_hbm, wv_ref)]
    out_copies = []

    lanes = lax.broadcasted_iota(jnp.int32, (2, HD), 1)
    for q in range(CHUNK):
        picked = chv_ref[q]
        found = jnp.full((2, HD), TOPK, jnp.int32)
        for n in range(TOPK):
            found = jnp.where(picked[:, n : n + 1] == lanes, n, found)
        names_ref[q] = found
        tm_ref[q, TOPK] = jnp.zeros((BLOCK, 2 * HD), BF16)

    pl.semaphore_wait(barrier, len(partners))
    names_copy = local(names_ref, inv_ref)

    units = [(g, kv) for g in range(2) for kv in range(2)]

    def slot(u, idx):
        g, kv = units[u]
        return kv_bufs[g][kv].at[pl.ds(pl.multiple_of(idx * CHUNK, CHUNK), CHUNK)]

    def put(u, idx, where):
        return plan(slot(u, idx), slot(u, idx), where)

    g_near, g_far, g_core, g_y = {}, {}, {}, {}
    for u in range(4):
        g_y[u] = put(u, c, to_y)
        for n, plane in enumerate((yh, py)):
            first = ctx_at(plane, x, k)
            g_near[u, n] = (put(u, first, to_right), put(u, first, to_left))
            if n == 1:
                g_far[u, n] = put(u, ctx_at(yh, xo, k), to_y)
            elif units[u][1] == 0:
                g_far[u, n] = put(u, ctx_at(plane, xl, k), to_right)
            else:
                g_far[u, n] = put(u, ctx_at(plane, xr, k), to_left)
            g_core[u, n] = [put(u, ctx_at(plane, xx, k), to_core) for xx in (x, xl, xr, xo)]

    def gather_first(u):
        for copy in own_copies[u]:
            copy.wait()
        g_near[u, 0][0].start()
        g_near[u, 0][1].start()
        g_core[u, 0][0].start()

    def gather_over(u):
        g_y[u].start()

    def gather_relay(u, n):
        for side in range(2):
            g_near[u, n][side].wait_recv()
            if n == 0 and units[u][1] == side:
                g_far[u, 0].start()
            g_core[u, n][1 + side].start()

    def gather_y(u):
        g_y[u].wait_recv()
        g_near[u, 1][0].start()
        g_near[u, 1][1].start()
        g_core[u, 1][0].start()

    def gather_far(u, n):
        g_far[u, n].wait_recv()
        if n == 0:
            g_far[u, 1].start()
        g_core[u, n][3].start()

    def gather_end(u):
        for n in range(2):
            for copy in g_core[u, n]:
                copy.wait_recv()

    def each(step, *names):
        for name in names:
            step(*name)

    for u in range(4):
        gather_first(u)
        gather_over(u)
    each(gather_relay, *((u, 0) for u in range(4)))
    each(gather_y, *((u,) for u in range(4)))
    each(gather_far, *((u, 0) for u in range(4)))
    each(gather_relay, (0, 1), (1, 1))
    each(gather_far, (0, 1), (1, 1))
    each(gather_end, (0,), (1,))
    for copy in query_copies:
        copy.wait()
    names_copy.wait()

    base = lax.broadcasted_iota(jnp.int32, (BLOCK, HD), 0) - (
        lax.broadcasted_iota(jnp.int32, (BLOCK, HD), 1) % BLOCK
    )

    def attend(g, q):
        own = c * CHUNK + q
        rows = pl.ds(pl.multiple_of(q * BLOCK, BLOCK), BLOCK)
        qb = jnp.concatenate([q_ref[rows, pl.ds((2 * g + i) * HD, HD)] for i in range(2)], axis=0)
        gb = jnp.concatenate([go_ref[rows, pl.ds((2 * g + i) * HD, HD)] for i in range(2)], axis=0)
        none = jnp.zeros((HD, HD), BF16)
        pair = jnp.concatenate(
            [jnp.concatenate([qb, none], axis=1), jnp.concatenate([none, gb], axis=1)], axis=0
        )
        blocks = [ch_ref[q, g, s] for s in range(TOPK)]
        kc = jnp.concatenate([kv_bufs[g][0][b] for b in blocks], axis=0)
        vc = jnp.concatenate([kv_bufs[g][1][b] for b in blocks], axis=0)
        lines = jnp.concatenate([kc, vc], axis=1)
        products = jnp.concatenate(
            [
                lax.dot_general(lines[:HALF_K], pair, NT, preferred_element_type=F32),
                lax.dot_general(lines[HALF_K:], pair, NT, preferred_element_type=F32),
            ],
            axis=0,
        )
        grad_w = products[:, HD:]
        scores = jnp.concatenate(
            [
                jnp.where(
                    base <= (own - blocks[s]) * BLOCK,
                    products[s * BLOCK : (s + 1) * BLOCK, :HD],
                    -1e30,
                )
                for s in range(TOPK)
            ],
            axis=0,
        )
        top = jnp.max(scores, axis=0, keepdims=True)
        weights = jnp.exp2((scores - top) * EXP2_SCALE)
        weights = weights * (1.0 / jnp.sum(weights, axis=0, keepdims=True))
        low = weights.astype(BF16)
        deltas = jnp.sum(low.astype(F32) * grad_w, axis=0, keepdims=True)
        grad_s = (weights * (grad_w - deltas)).astype(BF16)
        grad_q = SCALE * lax.dot_general(grad_s, kc, TN, preferred_element_type=F32)
        for i in range(2):
            gq_ref[rows, pl.ds((2 * g + i) * HD, HD)] = grad_q[i * BLOCK : (i + 1) * BLOCK].astype(BF16)
        lines = jnp.concatenate([grad_s, low], axis=1)
        term = jnp.concatenate(
            [
                jnp.dot(lines[:HALF_K], pair, preferred_element_type=F32),
                jnp.dot(lines[HALF_K:], pair, preferred_element_type=F32),
            ],
            axis=0,
        )
        for s in range(TOPK):
            part = term[s * BLOCK : (s + 1) * BLOCK]
            tm_ref[q, s, :, :HD] = (SCALE * part[:, :HD]).astype(BF16)
            tm_ref[q, s, :, HD:] = part[:, HD:].astype(BF16)

    def terms(g, plane):
        def body(i, carry):
            for b in range(2 * CHUNK):
                j = (plane * 4 + i) * (2 * CHUNK) + b
                total = tm_ref[0, inv_ref[0, g, j]].astype(F32)
                for q in range(1, CHUNK):
                    total = total + tm_ref[q, inv_ref[q, g, j]].astype(F32)
                total = total.astype(BF16)
                lines = pl.ds((b % CHUNK) * BLOCK, BLOCK)
                t_ref[2 * g, plane, b // CHUNK, i, lines, :] = total[:, :HD]
                t_ref[2 * g + 1, plane, b // CHUNK, i, lines, :] = total[:, HD:]
            return carry

        lax.fori_loop(0, 4, body, 0)

    planes = (py, yh)
    core_sums = {
        (u, n): plan(t_ref.at[u, planes[n], 1 - k], p_ref.at[u, planes[n]], to_core)
        for u in range(4)
        for n in range(2)
    }

    class Sum:
        def __init__(self, way, theirs, mine, bufs, places, ends, over):
            self.way, self.theirs, self.mine, self.bufs = way, theirs, mine, bufs
            self.here, right, left, across = places
            self.across = across
            go_right, go_left = ends
            first, far, l0, r0, l1, r1, stage, last = bufs
            self.first = plan(theirs.at[across], first, over)
            self.theirs_right = plan(theirs.at[right], l1, go_right)
            self.theirs_left = plan(theirs.at[left], r1, go_left)
            self.far = plan(mine.at[across], far, go_right if way == 0 else go_left)
            self.mine_right = plan(mine.at[right], l0, go_right)
            self.mine_left = plan(mine.at[left], r0, go_left)
            self.relayed, self.direct = (
                (self.mine_right, self.mine_left) if way == 0 else (self.mine_left, self.mine_right)
            )
            self.relay_at = right if way == 0 else left
            self.over = plan(stage, last, over)

        def start_theirs(self):
            self.first.start()
            self.theirs_right.start()
            self.theirs_left.start()

        def start_mine(self):
            self.direct.start()

        def add(self, i, buf):
            self.mine[i] = (self.mine[i].astype(F32) + buf[...].astype(F32)).astype(BF16)

        def go_far(self):
            self.first.wait_recv()
            self.add(self.across, self.bufs[0])
            self.far.start()

        def cross(self):
            _, _, _, _, l1, r1, stage, _ = self.bufs
            self.theirs_right.wait_recv()
            self.theirs_left.wait_recv()
            total = self.theirs[self.here].astype(F32) + l1[...].astype(F32) + r1[...].astype(F32)
            stage[...] = total.astype(BF16)
            self.over.start()

        def relay(self):
            self.far.wait_recv()
            self.add(self.relay_at, self.bufs[1])
            self.relayed.start()

        def end(self):
            _, _, l0, r0, _, _, _, last = self.bufs
            self.mine_right.wait_recv()
            self.mine_left.wait_recv()
            total = self.mine[self.here].astype(F32) + l0[...].astype(F32) + r0[...].astype(F32)
            self.over.wait_recv()
            return total + last[...].astype(F32)

    x_sums = [
        Sum(
            u % 2, s_ref.at[u, py], s_ref.at[u, yh],
            (xa_ref.at[u], xf_ref.at[u], xl_ref.at[u, 0], xr_ref.at[u, 0],
             xl_ref.at[u, 1], xr_ref.at[u, 1], xs_ref.at[u], xy_ref.at[u]),
            (x, xr, xl, xo), (to_right, to_left), to_y,
        )
        for u in range(4)
    ]

    def core_sum(u, n):
        plane = planes[n]
        core_sums[u, n].wait_recv()
        for xx in range(4):
            s_ref[u, plane, xx] = (
                t_ref[u, plane, k, xx].astype(F32) + p_ref[u, plane, xx].astype(F32)
            ).astype(BF16)
        if n == 0:
            x_sums[u].start_theirs()
        else:
            x_sums[u].start_mine()

    def sum_end(u):
        g, kv = units[u]
        (gk_ref, gv_ref)[kv][:, pl.ds(g * HD, HD)] = x_sums[u].end().astype(BF16)

    def do(names, *steps):
        for step in steps:
            for u in names:
                getattr(x_sums[u], step)()

    def core_start(g, n):
        core_sums[2 * g, n].start()
        core_sums[2 * g + 1, n].start()

    hooks = {
        (0, 1): lambda: each(gather_relay, (2, 1), (3, 1)),
        (0, 2): lambda: each(gather_far, (2, 1), (3, 1)),
        (1, 2): lambda: each(core_sum, (0, 0), (1, 0), (0, 1), (1, 1)),
    }
    for g in range(2):
        if g == 1:
            each(gather_end, (2,), (3,))

        def step(q, carry, g=g):
            for (gg, at), action in hooks.items():
                if gg == g:
                    pl.when(q == at)(lambda action=action: (action(), None)[1])
            attend(g, q)
            return carry

        lax.fori_loop(0, CHUNK, step, 0)
        if g == 1:
            out_copies.append(local(gq_ref, gq_hbm))
        for n in range(2):
            terms(g, planes[n])
            core_start(g, n)
    do((0, 1), "go_far")

    for copy in weight_copies:
        copy.wait()

    def query_part(i, carry):
        rows = pl.ds(pl.multiple_of(i * OUT_W, OUT_W), OUT_W)
        acc_ref[rows, :] = lax.dot_general(wq_ref[rows, :], gq_ref[...], NT, preferred_element_type=F32)
        return carry

    lax.fori_loop(0, 1, query_part, 0)
    each(core_sum, (2, 0), (3, 0))
    do((0, 1), "cross")
    each(core_sum, (2, 1), (3, 1))
    lax.fori_loop(1, 4, query_part, 0)
    do((0, 1), "relay")
    lax.fori_loop(4, 8, query_part, 0)
    do((2, 3), "go_far", "cross", "relay")
    each(sum_end, (0,), (1,), (2,), (3,))
    out_copies.append(local(gk_ref, gk_hbm))
    out_copies.append(local(gv_ref, gv_hbm))

    z_places = (z, zr, zl, zo)
    z_sums = [
        Sum(
            w, pt_ref.at[w, 1 - yl], pt_ref.at[w, yl],
            (za_ref.at[w], zf_ref.at[w], zl_ref.at[w, 0], zr_ref.at[w, 0],
             zl_ref.at[w, 1], zr_ref.at[w, 1], zs_ref.at[w], zy_ref.at[w]),
            z_places, (to_zr, to_zl), to_yl,
        )
        for w in range(2)
    ]

    def term_chunk(side, zz):
        i = zz * 2 + side
        rows = pl.ds(pl.multiple_of(i * OUT_W, OUT_W), OUT_W)
        out = acc_ref[rows, :]
        out = out + lax.dot_general(wk_ref[rows, :], gk_ref[...], NT, preferred_element_type=F32)
        out = out + lax.dot_general(wv_ref[rows, :], gv_ref[...], NT, preferred_element_type=F32)
        out = out.astype(BF16)
        for w in range(2):
            pt_ref[w, side, zz] = out[w * HALF_W : (w + 1) * HALF_W]

    def both(step):
        for w in range(2):
            step(z_sums[w])

    term_chunk(1 - yl, zo)
    both(lambda t: t.first.start())
    term_chunk(1 - yl, zr)
    both(lambda t: t.theirs_right.start())
    term_chunk(1 - yl, zl)
    both(lambda t: t.theirs_left.start())
    term_chunk(yl, zo)
    term_chunk(yl, zl)
    term_chunk(yl, zr)
    both(lambda t: (t.go_far(), t.start_mine()))
    term_chunk(1 - yl, z)
    term_chunk(yl, z)
    both(lambda t: t.cross())
    both(lambda t: t.relay())
    for w in range(2):
        gi_ref[pl.ds(w * HALF_W, HALF_W), :] = z_sums[w].end().astype(BF16)
        out_copies.append(
            local(gi_ref.at[pl.ds(w * HALF_W, HALF_W)], gi_hbm.at[pl.ds(w * HALF_W, HALF_W)])
        )

    for copy in out_copies:
        copy.wait()
    for copy in started:
        copy.wait_send()


def write_out(*refs):
    for src, dst in zip(refs[:4], refs[4:]):
        dst[...] = src[...]


def body(queries, keys, values, grad_out, chosen, w_query, w_key, w_value):
    vmem = pl.BlockSpec(memory_space=pltpu.VMEM)
    smem = pl.BlockSpec(memory_space=pltpu.SMEM)
    hbm = pl.BlockSpec(memory_space=pl.ANY)
    shape = jax.ShapeDtypeStruct
    buf = lambda *dims: pltpu.VMEM(dims, BF16)
    chunk = (ROWS, HD)
    zc = (HALF_W, ROWS)
    outs = pl.pallas_call(
        kernel,
        out_shape=(
            shape((ROWS, 512), BF16),
            shape((ROWS, 256), BF16),
            shape((ROWS, 256), BF16),
            shape((OUT_W, ROWS), BF16),
        ),
        in_specs=[hbm, hbm, hbm, hbm, smem, vmem, hbm, hbm, hbm],
        out_specs=(hbm,) * 4,
        scratch_shapes=[
            buf(64, BLOCK, HD), buf(64, BLOCK, HD), buf(64, BLOCK, HD), buf(64, BLOCK, HD),
            buf(ROWS, 512), buf(ROWS, 512), buf(ROWS, 512), buf(ROWS, 256), buf(ROWS, 256), buf(OUT_W, ROWS),
            buf(CHUNK, TOPK + 1, BLOCK, 2 * HD),
            pltpu.VMEM((CHUNK, 2, HD), jnp.int32), pltpu.SMEM((CHUNK, 2, HD), jnp.int32),
            buf(4, 2, 2, 4, *chunk), buf(4, 2, 4, *chunk), buf(4, 2, 4, *chunk),
            buf(4, *chunk), buf(4, *chunk), buf(4, 2, *chunk), buf(4, 2, *chunk), buf(4, *chunk), buf(4, *chunk),
            buf(4608, 512), buf(4608, 256), buf(4608, 256), pltpu.VMEM((4608, ROWS), F32),
            buf(2, 2, 4, *zc), buf(2, *zc), buf(2, *zc),
            buf(2, 2, *zc), buf(2, 2, *zc), buf(2, *zc), buf(2, *zc),
            pltpu.SemaphoreType.DMA((N_COPIES,)),
            pltpu.SemaphoreType.DMA((N_COPIES,)),
            pltpu.SemaphoreType.DMA((32,)),
        ],
        compiler_params=pltpu.CompilerParams(
            collective_id=0, has_side_effects=True, vmem_limit_bytes=60 * 1024 * 1024
        ),
    )(queries, grad_out, keys, values, chosen, chosen, w_query, w_key, w_value)
    grad_queries, grad_keys, grad_values, grad_input = pl.pallas_call(
        write_out,
        out_shape=tuple(shape(o.shape, o.dtype) for o in outs),
        in_specs=[vmem] * 4,
        out_specs=(vmem,) * 4,
    )(*outs)
    return grad_queries, grad_keys, grad_values, grad_input.T


def solution(mesh):
    both = P("ctx", "head")
    return jax.shard_map(
        body,
        mesh=mesh,
        in_specs=(both, both, both, both, P("ctx", "head", None)) + (P(None, "head"),) * 3,
        out_specs=(both, both, both, both),
        check_vma=False,
    )
```

```python
import functools
import math

import jax
import jax.numpy as jnp
from jax import lax
from jax.experimental import pallas as pl
from jax.experimental.pallas import tpu as pltpu
from jax.sharding import PartitionSpec as P

HD = 128
BLOCK = 64
TOPK = 16
NX = 4
ROWS = 256
CHUNK = 4
OUT_W = 576
HALF_W = OUT_W // 2
HALF_K = TOPK * BLOCK // 2
SCALE = 1.0 / math.sqrt(HD)
EXP2_SCALE = SCALE / math.log(2.0)
NT = (((1,), (1,)), ((), ()))
TN = (((0,), (0,)), ((), ()))
F32 = jnp.float32
BF16 = jnp.bfloat16
N_COPIES = 184


def kernel(
    q_hbm, go_hbm, k_hbm, v_hbm, ch_ref, chv_ref, wq_hbm, wk_hbm, wv_hbm,
    gq_hbm, gk_hbm, gv_hbm, gi_hbm,
    kv00, kv01, kv10, kv11, q_ref, go_ref, gq_ref, gk_ref, gv_ref, gi_ref,
    tm_ref, names_ref, inv_ref,
    t_ref, p_ref, s_ref, xa_ref, xf_ref, xl_ref, xr_ref, xs_ref, xy_ref,
    wq_ref, wk_ref, wv_ref, acc_ref, pt_ref, za_ref, zf_ref, zl_ref, zr_ref, zs_ref, zy_ref,
    send_sem, recv_sem, local_sem,
):
    c = lax.axis_index("ctx")
    h = lax.axis_index("head")
    yh, x, k = c // 8, (c // 2) % 4, c % 2
    z, yl = h // 2, h % 2
    kv_bufs = ((kv00, kv01), (kv10, kv11))

    def ctx_at(p, xx, kk):
        return p * 8 + xx * 2 + kk

    xr, xl, xo = (x + 1) % 4, (x + 3) % 4, (x + 2) % 4
    zr, zl, zo = (z + 1) % 4, (z + 3) % 4, (z + 2) % 4
    py = 1 - yh
    to_right = (ctx_at(yh, xr, k), h)
    to_left = (ctx_at(yh, xl, k), h)
    to_y = (ctx_at(py, x, k), h)
    to_core = (ctx_at(yh, x, 1 - k), h)
    to_zr = (c, zr * 2 + yl)
    to_zl = (c, zl * 2 + yl)
    to_yl = (c, z * 2 + (1 - yl))

    started = []

    def plan(src, dst, where):
        i = len(started)
        copy = pltpu.make_async_remote_copy(
            src_ref=src,
            dst_ref=dst,
            send_sem=send_sem.at[i],
            recv_sem=recv_sem.at[i],
            device_id=where,
            device_id_type=pl.DeviceIdType.MESH,
        )
        started.append(copy)
        return copy

    def send(src, dst, where):
        copy = plan(src, dst, where)
        copy.start()
        return copy

    barrier = pltpu.get_barrier_semaphore()
    partners = (to_right, to_left, to_y, to_core, to_zr, to_zl, to_yl)
    for where in partners:
        pl.semaphore_signal(barrier, inc=1, device_id=where, device_id_type=pl.DeviceIdType.MESH)

    own_copies = []
    n_local = 0
    for g in range(2):
        for kv in range(2):
            src = (k_hbm, v_hbm)[kv]
            group = []
            for b in range(CHUNK):
                copy = pltpu.make_async_copy(
                    src.at[pl.ds(b * BLOCK, BLOCK), pl.ds(g * HD, HD)],
                    kv_bufs[g][kv].at[c * CHUNK + b],
                    local_sem.at[n_local],
                )
                n_local += 1
                copy.start()
                group.append(copy)
            own_copies.append(group)

    def local(src, dst):
        nonlocal n_local
        copy = pltpu.make_async_copy(src, dst, local_sem.at[n_local])
        n_local += 1
        copy.start()
        return copy

    query_copies = [local(q_hbm, q_ref), local(go_hbm, go_ref)]
    weight_copies = [local(wq_hbm, wq_ref), local(wk_hbm, wk_ref), local(wv_hbm, wv_ref)]
    out_copies = []

    lanes = lax.broadcasted_iota(jnp.int32, (2, HD), 1)
    for q in range(CHUNK):
        picked = chv_ref[q]
        found = jnp.full((2, HD), TOPK, jnp.int32)
        for n in range(TOPK):
            found = jnp.where(picked[:, n : n + 1] == lanes, n, found)
        names_ref[q] = found
        tm_ref[q, TOPK] = jnp.zeros((BLOCK, 2 * HD), BF16)

    pl.semaphore_wait(barrier, len(partners))
    names_copy = local(names_ref, inv_ref)

    units = [(g, kv) for g in range(2) for kv in range(2)]

    def slot(u, idx):
        g, kv = units[u]
        return kv_bufs[g][kv].at[pl.ds(pl.multiple_of(idx * CHUNK, CHUNK), CHUNK)]

    def put(u, idx, where):
        return plan(slot(u, idx), slot(u, idx), where)

    g_near, g_far, g_core, g_y = {}, {}, {}, {}
    for u in range(4):
        g_y[u] = put(u, c, to_y)
        for n, plane in enumerate((yh, py)):
            first = ctx_at(plane, x, k)
            g_near[u, n] = (put(u, first, to_right), put(u, first, to_left))
            if n == 1:
                g_far[u, n] = put(u, ctx_at(yh, xo, k), to_y)
            elif units[u][1] == 0:
                g_far[u, n] = put(u, ctx_at(plane, xl, k), to_right)
            else:
                g_far[u, n] = put(u, ctx_at(plane, xr, k), to_left)
            g_core[u, n] = [put(u, ctx_at(plane, xx, k), to_core) for xx in (x, xl, xr, xo)]

    def gather_first(u):
        for copy in own_copies[u]:
            copy.wait()
        g_near[u, 0][0].start()
        g_near[u, 0][1].start()
        g_core[u, 0][0].start()

    def gather_over(u):
        g_y[u].start()

    def gather_relay(u, n):
        for side in range(2):
            g_near[u, n][side].wait_recv()
            if n == 0 and units[u][1] == side:
                g_far[u, 0].start()
            g_core[u, n][1 + side].start()

    def gather_y(u):
        g_y[u].wait_recv()
        g_near[u, 1][0].start()
        g_near[u, 1][1].start()
        g_core[u, 1][0].start()

    def gather_far(u, n):
        g_far[u, n].wait_recv()
        if n == 0:
            g_far[u, 1].start()
        g_core[u, n][3].start()

    def gather_end(u):
        for n in range(2):
            for copy in g_core[u, n]:
                copy.wait_recv()

    def each(step, *names):
        for name in names:
            step(*name)

    for u in range(4):
        gather_first(u)
        gather_over(u)
    each(gather_relay, *((u, 0) for u in range(4)))
    each(gather_y, *((u,) for u in range(4)))
    each(gather_far, *((u, 0) for u in range(4)))
    each(gather_relay, (0, 1), (1, 1))
    each(gather_far, (0, 1), (1, 1))
    each(gather_end, (0,), (1,))
    for copy in query_copies:
        copy.wait()
    names_copy.wait()

    base = lax.broadcasted_iota(jnp.int32, (BLOCK, HD), 0) - (
        lax.broadcasted_iota(jnp.int32, (BLOCK, HD), 1) % BLOCK
    )

    def attend(g, q):
        own = c * CHUNK + q
        rows = pl.ds(pl.multiple_of(q * BLOCK, BLOCK), BLOCK)
        qb = jnp.concatenate([q_ref[rows, pl.ds((2 * g + i) * HD, HD)] for i in range(2)], axis=0)
        gb = jnp.concatenate([go_ref[rows, pl.ds((2 * g + i) * HD, HD)] for i in range(2)], axis=0)
        none = jnp.zeros((HD, HD), BF16)
        pair = jnp.concatenate(
            [jnp.concatenate([qb, none], axis=1), jnp.concatenate([none, gb], axis=1)], axis=0
        )
        blocks = [ch_ref[q, g, s] for s in range(TOPK)]
        kc = jnp.concatenate([kv_bufs[g][0][b] for b in blocks], axis=0)
        vc = jnp.concatenate([kv_bufs[g][1][b] for b in blocks], axis=0)
        lines = jnp.concatenate([kc, vc], axis=1)
        products = jnp.concatenate(
            [
                lax.dot_general(lines[:HALF_K], pair, NT, preferred_element_type=F32),
                lax.dot_general(lines[HALF_K:], pair, NT, preferred_element_type=F32),
            ],
            axis=0,
        )
        grad_w = products[:, HD:]
        scores = jnp.concatenate(
            [
                jnp.where(
                    base <= (own - blocks[s]) * BLOCK,
                    products[s * BLOCK : (s + 1) * BLOCK, :HD],
                    -1e30,
                )
                for s in range(TOPK)
            ],
            axis=0,
        )
        top = jnp.max(scores, axis=0, keepdims=True)
        weights = jnp.exp2((scores - top) * EXP2_SCALE)
        weights = weights * (1.0 / jnp.sum(weights, axis=0, keepdims=True))
        low = weights.astype(BF16)
        deltas = jnp.sum(low.astype(F32) * grad_w, axis=0, keepdims=True)
        grad_s = (weights * (grad_w - deltas)).astype(BF16)
        grad_q = SCALE * lax.dot_general(grad_s, kc, TN, preferred_element_type=F32)
        for i in range(2):
            gq_ref[rows, pl.ds((2 * g + i) * HD, HD)] = grad_q[i * BLOCK : (i + 1) * BLOCK].astype(BF16)
        lines = jnp.concatenate([grad_s, low], axis=1)
        term = jnp.concatenate(
            [
                jnp.dot(lines[:HALF_K], pair, preferred_element_type=F32),
                jnp.dot(lines[HALF_K:], pair, preferred_element_type=F32),
            ],
            axis=0,
        )
        for s in range(TOPK):
            part = term[s * BLOCK : (s + 1) * BLOCK]
            tm_ref[q, s, :, :HD] = (SCALE * part[:, :HD]).astype(BF16)
            tm_ref[q, s, :, HD:] = part[:, HD:].astype(BF16)

    def terms(g, plane):
        def body(i, carry):
            for b in range(2 * CHUNK):
                j = (plane * 4 + i) * (2 * CHUNK) + b
                total = tm_ref[0, inv_ref[0, g, j]].astype(F32)
                for q in range(1, CHUNK):
                    total = total + tm_ref[q, inv_ref[q, g, j]].astype(F32)
                total = total.astype(BF16)
                lines = pl.ds((b % CHUNK) * BLOCK, BLOCK)
                t_ref[2 * g, plane, b // CHUNK, i, lines, :] = total[:, :HD]
                t_ref[2 * g + 1, plane, b // CHUNK, i, lines, :] = total[:, HD:]
            return carry

        lax.fori_loop(0, 4, body, 0)

    planes = (py, yh)
    core_sums = {
        (u, n): plan(t_ref.at[u, planes[n], 1 - k], p_ref.at[u, planes[n]], to_core)
        for u in range(4)
        for n in range(2)
    }

    class Sum:
        def __init__(self, way, theirs, mine, bufs, places, ends, over):
            self.way, self.theirs, self.mine, self.bufs = way, theirs, mine, bufs
            self.here, right, left, across = places
            self.across = across
            go_right, go_left = ends
            first, far, l0, r0, l1, r1, stage, last = bufs
            self.first = plan(theirs.at[across], first, over)
            self.theirs_right = plan(theirs.at[right], l1, go_right)
            self.theirs_left = plan(theirs.at[left], r1, go_left)
            self.far = plan(mine.at[across], far, go_right if way == 0 else go_left)
            self.mine_right = plan(mine.at[right], l0, go_right)
            self.mine_left = plan(mine.at[left], r0, go_left)
            self.relayed, self.direct = (
                (self.mine_right, self.mine_left) if way == 0 else (self.mine_left, self.mine_right)
            )
            self.relay_at = right if way == 0 else left
            self.over = plan(stage, last, over)

        def start_first(self):
            self.first.start()

        def start_near(self):
            self.theirs_right.start()
            self.theirs_left.start()

        def start_theirs(self):
            self.start_first()
            self.start_near()

        def start_mine(self):
            self.direct.start()

        def add(self, i, buf):
            self.mine[i] = (self.mine[i].astype(F32) + buf[...].astype(F32)).astype(BF16)

        def go_far(self):
            self.first.wait_recv()
            self.add(self.across, self.bufs[0])
            self.far.start()

        def cross(self):
            _, _, _, _, l1, r1, stage, _ = self.bufs
            self.theirs_right.wait_recv()
            self.theirs_left.wait_recv()
            total = self.theirs[self.here].astype(F32) + l1[...].astype(F32) + r1[...].astype(F32)
            stage[...] = total.astype(BF16)
            self.over.start()

        def relay(self):
            self.far.wait_recv()
            self.add(self.relay_at, self.bufs[1])
            self.relayed.start()

        def end(self):
            _, _, l0, r0, _, _, _, last = self.bufs
            self.mine_right.wait_recv()
            self.mine_left.wait_recv()
            total = self.mine[self.here].astype(F32) + l0[...].astype(F32) + r0[...].astype(F32)
            self.over.wait_recv()
            return total + last[...].astype(F32)

    x_sums = {
        (u, e): Sum(
            u % 2, s_ref.at[u, e, py], s_ref.at[u, e, yh],
            (xa_ref.at[u, e], xf_ref.at[u, e], xl_ref.at[u, e, 0], xr_ref.at[u, e, 0],
             xl_ref.at[u, e, 1], xr_ref.at[u, e, 1], xs_ref.at[u, e], xy_ref.at[u, e]),
            (x, xr, xl, xo), (to_right, to_left), to_y,
        )
        for u in range(4)
        for e in range(2)
    }

    def core_sum(u, n):
        plane = planes[n]
        core_sums[u, n].wait_recv()
        for e in range(2):
            half = pl.ds(e * HD, HD)
            for xx in range(4):
                s_ref[u, e, plane, xx] = (
                    t_ref[u, plane, k, xx, half, :].astype(F32) + p_ref[u, plane, xx, half, :].astype(F32)
                ).astype(BF16)

    def sum_end(u, e):
        g, kv = units[u]
        (gk_ref, gv_ref)[kv][pl.ds(e * HD, HD), pl.ds(g * HD, HD)] = x_sums[u, e].end().astype(BF16)

    def do(names, *steps):
        for step in steps:
            for name in names:
                getattr(x_sums[name], step)()

    def core_start(g, n):
        core_sums[2 * g, n].start()
        core_sums[2 * g + 1, n].start()

    LOW = [[(0, e), (1, e)] for e in range(2)]
    HIGH = [[(2, e), (3, e)] for e in range(2)]
    hooks = {
        (0, 1): lambda: each(gather_relay, (2, 1), (3, 1)),
        (0, 2): lambda: each(gather_far, (2, 1), (3, 1)),
        (1, 2): lambda: (
            each(core_sum, (0, 0), (1, 0)),
            do(LOW[0] + LOW[1], "start_theirs"),
            each(core_sum, (0, 1), (1, 1)),
            do(LOW[0] + LOW[1], "start_mine"),
        ),
    }
    for g in range(2):
        if g == 1:
            each(gather_end, (2,), (3,))

        def step(q, carry, g=g):
            for (gg, at), action in hooks.items():
                if gg == g:
                    pl.when(q == at)(lambda action=action: (action(), None)[1])
            attend(g, q)
            return carry

        lax.fori_loop(0, CHUNK, step, 0)
        if g == 1:
            out_copies.append(local(gq_ref, gq_hbm))
        for n in range(2):
            terms(g, planes[n])
            core_start(g, n)
    do(LOW[0] + LOW[1], "go_far")

    for copy in weight_copies:
        copy.wait()

    def query_part(i, carry):
        rows = pl.ds(pl.multiple_of(i * OUT_W, OUT_W), OUT_W)
        acc_ref[rows, :] = lax.dot_general(wq_ref[rows, :], gq_ref[...], NT, preferred_element_type=F32)
        return carry

    each(core_sum, (2, 0), (3, 0))
    do(HIGH[0], "start_theirs")
    do(HIGH[1], "start_first")
    each(core_sum, (2, 1), (3, 1))
    do(LOW[0], "cross")
    lax.fori_loop(0, 4, query_part, 0)
    do(LOW[0] + LOW[1], "relay")
    lax.fori_loop(4, 5, query_part, 0)
    do(HIGH[0], "go_far", "start_mine", "cross")
    do(LOW[1], "cross")
    do(HIGH[1][:1], "start_near")
    lax.fori_loop(5, 8, query_part, 0)
    do(HIGH[0], "relay")
    do(HIGH[1][1:], "start_near")
    do(HIGH[1], "go_far", "start_mine")
    each(sum_end, *((u, 0) for u in range(4)))

    z_places = (z, zr, zl, zo)
    z_sums = {
        (e, w): Sum(
            w, pt_ref.at[e, w, 1 - yl], pt_ref.at[e, w, yl],
            (za_ref.at[e, w], zf_ref.at[e, w], zl_ref.at[e, w, 0], zr_ref.at[e, w, 0],
             zl_ref.at[e, w, 1], zr_ref.at[e, w, 1], zs_ref.at[e, w], zy_ref.at[e, w]),
            z_places, (to_zr, to_zl), to_yl,
        )
        for e in range(2)
        for w in range(2)
    }

    def term_chunk(e, side, zz):
        i = zz * 2 + side
        rows = pl.ds(pl.multiple_of(i * OUT_W, OUT_W), OUT_W)
        half = pl.ds(e * HD, HD)
        out = acc_ref[rows, half]
        out = out + lax.dot_general(wk_ref[rows, :], gk_ref[half, :], NT, preferred_element_type=F32)
        out = out + lax.dot_general(wv_ref[rows, :], gv_ref[half, :], NT, preferred_element_type=F32)
        out = out.astype(BF16)
        for w in range(2):
            pt_ref[e, w, side, zz] = out[w * HALF_W : (w + 1) * HALF_W]

    def both(e, step):
        for w in range(2):
            step(z_sums[e, w])

    def send_theirs(e):
        term_chunk(e, 1 - yl, zo)
        both(e, lambda t: t.first.start())
        term_chunk(e, 1 - yl, zr)
        both(e, lambda t: t.theirs_right.start())
        term_chunk(e, 1 - yl, zl)
        both(e, lambda t: t.theirs_left.start())

    def own_chunks(e):
        for zz in (zo, zl, zr):
            term_chunk(e, yl, zz)

    def last_chunks(e):
        term_chunk(e, 1 - yl, z)
        term_chunk(e, yl, z)

    def z_end(e):
        for w in range(2):
            gi_ref[pl.ds(w * HALF_W, HALF_W), pl.ds(e * HD, HD)] = z_sums[e, w].end().astype(BF16)

    send_theirs(0)
    do(HIGH[1], "cross")
    own_chunks(0)
    do(HIGH[1], "relay")
    last_chunks(0)
    both(0, lambda t: (t.go_far(), t.start_mine()))
    each(sum_end, *((u, 1) for u in range(4)))
    out_copies.append(local(gk_ref, gk_hbm))
    out_copies.append(local(gv_ref, gv_hbm))
    send_theirs(1)
    own_chunks(1)
    last_chunks(1)
    both(0, lambda t: t.cross())
    both(1, lambda t: (t.go_far(), t.start_mine()))
    both(0, lambda t: t.relay())
    both(1, lambda t: t.cross())
    both(1, lambda t: t.relay())
    z_end(0)
    z_end(1)
    out_copies.append(local(gi_ref, gi_hbm))

    for copy in out_copies:
        copy.wait()
    for copy in started:
        copy.wait_send()


def write_out(*refs):
    for src, dst in zip(refs[:4], refs[4:]):
        dst[...] = src[...]


def body(queries, keys, values, grad_out, chosen, w_query, w_key, w_value):
    vmem = pl.BlockSpec(memory_space=pltpu.VMEM)
    smem = pl.BlockSpec(memory_space=pltpu.SMEM)
    hbm = pl.BlockSpec(memory_space=pl.ANY)
    shape = jax.ShapeDtypeStruct
    buf = lambda *dims: pltpu.VMEM(dims, BF16)
    chunk = (ROWS, HD)
    zc = (2, HALF_W, HD)
    outs = pl.pallas_call(
        kernel,
        out_shape=(
            shape((ROWS, 512), BF16),
            shape((ROWS, 256), BF16),
            shape((ROWS, 256), BF16),
            shape((OUT_W, ROWS), BF16),
        ),
        in_specs=[hbm, hbm, hbm, hbm, smem, vmem, hbm, hbm, hbm],
        out_specs=(hbm,) * 4,
        scratch_shapes=[
            buf(64, BLOCK, HD), buf(64, BLOCK, HD), buf(64, BLOCK, HD), buf(64, BLOCK, HD),
            buf(ROWS, 512), buf(ROWS, 512), buf(ROWS, 512), buf(ROWS, 256), buf(ROWS, 256), buf(OUT_W, ROWS),
            buf(CHUNK, TOPK + 1, BLOCK, 2 * HD),
            pltpu.VMEM((CHUNK, 2, HD), jnp.int32), pltpu.SMEM((CHUNK, 2, HD), jnp.int32),
            buf(4, 2, 2, 4, *chunk), buf(4, 2, 4, *chunk), buf(4, 2, 2, 4, HD, HD),
            buf(4, 2, HD, HD), buf(4, 2, HD, HD), buf(4, 2, 2, HD, HD), buf(4, 2, 2, HD, HD), buf(4, 2, HD, HD), buf(4, 2, HD, HD),
            buf(4608, 512), buf(4608, 256), buf(4608, 256), pltpu.VMEM((4608, ROWS), F32),
            buf(2, 2, 2, 4, HALF_W, HD), buf(2, *zc), buf(2, *zc),
            buf(2, 2, 2, HALF_W, HD), buf(2, 2, 2, HALF_W, HD), buf(2, *zc), buf(2, *zc),
            pltpu.SemaphoreType.DMA((N_COPIES,)),
            pltpu.SemaphoreType.DMA((N_COPIES,)),
            pltpu.SemaphoreType.DMA((32,)),
        ],
        compiler_params=pltpu.CompilerParams(
            collective_id=0, has_side_effects=True, vmem_limit_bytes=60 * 1024 * 1024
        ),
    )(queries, grad_out, keys, values, chosen, chosen, w_query, w_key, w_value)
    grad_queries, grad_keys, grad_values, grad_input = pl.pallas_call(
        write_out,
        out_shape=tuple(shape(o.shape, o.dtype) for o in outs),
        in_specs=[vmem] * 4,
        out_specs=(vmem,) * 4,
    )(*outs)
    return grad_queries, grad_keys, grad_values, grad_input.T


def solution(mesh):
    both = P("ctx", "head")
    return jax.shard_map(
        body,
        mesh=mesh,
        in_specs=(both, both, both, both, P("ctx", "head", None)) + (P(None, "head"),) * 3,
        out_specs=(both, both, both, both),
        check_vma=False,
    )
```

```python
import functools
import math

import jax
import jax.numpy as jnp
from jax import lax
from jax.experimental import pallas as pl
from jax.experimental.pallas import tpu as pltpu
from jax.sharding import PartitionSpec as P

HD = 128
BLOCK = 64
TOPK = 16
NX = 4
ROWS = 256
CHUNK = 4
OUT_W = 576
HALF_W = OUT_W // 2
HALF_K = TOPK * BLOCK // 2
SCALE = 1.0 / math.sqrt(HD)
EXP2_SCALE = SCALE / math.log(2.0)
NT = (((1,), (1,)), ((), ()))
TN = (((0,), (0,)), ((), ()))
F32 = jnp.float32
BF16 = jnp.bfloat16
N_COPIES = 184


def kernel(
    q_hbm, go_hbm, k_hbm, v_hbm, ch_hbm, wq_hbm, wk_hbm, wv_hbm,
    gq_hbm, gk_hbm, gv_hbm, gi_hbm,
    kv00, kv01, kv10, kv11, q_ref, go_ref, gq_ref, gk_ref, gv_ref, gi_ref,
    tm_ref, ch_ref, chv_ref, names_ref, inv_ref,
    t_ref, p_ref, s_ref, xa_ref, xf_ref, xl_ref, xr_ref, xs_ref, xy_ref,
    wq_ref, wk_ref, wv_ref, acc_ref, pt_ref, za_ref, zf_ref, zl_ref, zr_ref, zs_ref, zy_ref,
    send_sem, recv_sem, local_sem,
):
    c = lax.axis_index("ctx")
    h = lax.axis_index("head")
    yh, x, k = c // 8, (c // 2) % 4, c % 2
    z, yl = h // 2, h % 2
    kv_bufs = ((kv00, kv01), (kv10, kv11))

    def ctx_at(p, xx, kk):
        return p * 8 + xx * 2 + kk

    xr, xl, xo = (x + 1) % 4, (x + 3) % 4, (x + 2) % 4
    zr, zl, zo = (z + 1) % 4, (z + 3) % 4, (z + 2) % 4
    py = 1 - yh
    to_right = (ctx_at(yh, xr, k), h)
    to_left = (ctx_at(yh, xl, k), h)
    to_y = (ctx_at(py, x, k), h)
    to_core = (ctx_at(yh, x, 1 - k), h)
    to_zr = (c, zr * 2 + yl)
    to_zl = (c, zl * 2 + yl)
    to_yl = (c, z * 2 + (1 - yl))

    started = []

    def plan(src, dst, where):
        i = len(started)
        copy = pltpu.make_async_remote_copy(
            src_ref=src,
            dst_ref=dst,
            send_sem=send_sem.at[i],
            recv_sem=recv_sem.at[i],
            device_id=where,
            device_id_type=pl.DeviceIdType.MESH,
        )
        started.append(copy)
        return copy

    def send(src, dst, where):
        copy = plan(src, dst, where)
        copy.start()
        return copy

    barrier = pltpu.get_barrier_semaphore()
    partners = (to_right, to_left, to_y, to_core, to_zr, to_zl, to_yl)
    for where in partners:
        pl.semaphore_signal(barrier, inc=1, device_id=where, device_id_type=pl.DeviceIdType.MESH)

    own_copies = []
    choice_copies = [
        pltpu.make_async_copy(ch_hbm, chv_ref, local_sem.at[30]),
        pltpu.make_async_copy(ch_hbm, ch_ref, local_sem.at[31]),
    ]
    for copy in choice_copies:
        copy.start()
    n_local = 0
    for g in range(2):
        for kv in range(2):
            src = (k_hbm, v_hbm)[kv]
            group = []
            for b in range(CHUNK):
                copy = pltpu.make_async_copy(
                    src.at[pl.ds(b * BLOCK, BLOCK), pl.ds(g * HD, HD)],
                    kv_bufs[g][kv].at[c * CHUNK + b],
                    local_sem.at[n_local],
                )
                n_local += 1
                copy.start()
                group.append(copy)
            own_copies.append(group)

    def local(src, dst):
        nonlocal n_local
        copy = pltpu.make_async_copy(src, dst, local_sem.at[n_local])
        n_local += 1
        copy.start()
        return copy

    query_copies = [local(q_hbm, q_ref), local(go_hbm, go_ref)]
    weight_copies = [local(wq_hbm, wq_ref), local(wk_hbm, wk_ref), local(wv_hbm, wv_ref)]
    out_copies = []

    for copy in choice_copies:
        copy.wait()
    lanes = lax.broadcasted_iota(jnp.int32, (2, HD), 1)
    for q in range(CHUNK):
        picked = chv_ref[q]
        found = jnp.full((2, HD), TOPK, jnp.int32)
        for n in range(TOPK):
            found = jnp.where(picked[:, n : n + 1] == lanes, n, found)
        names_ref[q] = found
        tm_ref[q, TOPK] = jnp.zeros((BLOCK, 2 * HD), BF16)

    pl.semaphore_wait(barrier, len(partners))
    names_copy = local(names_ref, inv_ref)

    units = [(g, kv) for g in range(2) for kv in range(2)]

    def slot(u, idx):
        g, kv = units[u]
        return kv_bufs[g][kv].at[pl.ds(pl.multiple_of(idx * CHUNK, CHUNK), CHUNK)]

    def put(u, idx, where):
        return plan(slot(u, idx), slot(u, idx), where)

    g_near, g_far, g_core, g_y = {}, {}, {}, {}
    for u in range(4):
        g_y[u] = put(u, c, to_y)
        for n, plane in enumerate((yh, py)):
            first = ctx_at(plane, x, k)
            g_near[u, n] = (put(u, first, to_right), put(u, first, to_left))
            if n == 1:
                g_far[u, n] = put(u, ctx_at(yh, xo, k), to_y)
            elif units[u][1] == 0:
                g_far[u, n] = put(u, ctx_at(plane, xl, k), to_right)
            else:
                g_far[u, n] = put(u, ctx_at(plane, xr, k), to_left)
            g_core[u, n] = [put(u, ctx_at(plane, xx, k), to_core) for xx in (x, xl, xr, xo)]

    def gather_first(u):
        for copy in own_copies[u]:
            copy.wait()
        g_near[u, 0][0].start()
        g_near[u, 0][1].start()
        g_core[u, 0][0].start()

    def gather_over(u):
        g_y[u].start()

    def gather_relay(u, n):
        for side in range(2):
            g_near[u, n][side].wait_recv()
            if n == 0 and units[u][1] == side:
                g_far[u, 0].start()
            g_core[u, n][1 + side].start()

    def gather_y(u):
        g_y[u].wait_recv()
        g_near[u, 1][0].start()
        g_near[u, 1][1].start()
        g_core[u, 1][0].start()

    def gather_far(u, n):
        g_far[u, n].wait_recv()
        if n == 0:
            g_far[u, 1].start()
        g_core[u, n][3].start()

    def gather_end(u):
        for n in range(2):
            for copy in g_core[u, n]:
                copy.wait_recv()

    def each(step, *names):
        for name in names:
            step(*name)

    for u in range(4):
        gather_first(u)
        gather_over(u)
    each(gather_relay, *((u, 0) for u in range(4)))
    each(gather_y, *((u,) for u in range(4)))
    each(gather_far, *((u, 0) for u in range(4)))
    each(gather_relay, (0, 1), (1, 1))
    each(gather_far, (0, 1), (1, 1))
    each(gather_end, (0,), (1,))
    for copy in query_copies:
        copy.wait()
    names_copy.wait()

    base = lax.broadcasted_iota(jnp.int32, (BLOCK, HD), 0) - (
        lax.broadcasted_iota(jnp.int32, (BLOCK, HD), 1) % BLOCK
    )

    def attend(g, q):
        own = c * CHUNK + q
        rows = pl.ds(pl.multiple_of(q * BLOCK, BLOCK), BLOCK)
        qb = jnp.concatenate([q_ref[rows, pl.ds((2 * g + i) * HD, HD)] for i in range(2)], axis=0)
        gb = jnp.concatenate([go_ref[rows, pl.ds((2 * g + i) * HD, HD)] for i in range(2)], axis=0)
        none = jnp.zeros((HD, HD), BF16)
        pair = jnp.concatenate(
            [jnp.concatenate([qb, none], axis=1), jnp.concatenate([none, gb], axis=1)], axis=0
        )
        blocks = [ch_ref[q, g, s] for s in range(TOPK)]
        kc = jnp.concatenate([kv_bufs[g][0][b] for b in blocks], axis=0)
        vc = jnp.concatenate([kv_bufs[g][1][b] for b in blocks], axis=0)
        lines = jnp.concatenate([kc, vc], axis=1)
        products = jnp.concatenate(
            [
                lax.dot_general(lines[:HALF_K], pair, NT, preferred_element_type=F32),
                lax.dot_general(lines[HALF_K:], pair, NT, preferred_element_type=F32),
            ],
            axis=0,
        )
        grad_w = products[:, HD:]
        scores = jnp.concatenate(
            [
                jnp.where(
                    base <= (own - blocks[s]) * BLOCK,
                    products[s * BLOCK : (s + 1) * BLOCK, :HD],
                    -1e30,
                )
                for s in range(TOPK)
            ],
            axis=0,
        )
        top = jnp.max(scores, axis=0, keepdims=True)
        weights = jnp.exp2((scores - top) * EXP2_SCALE)
        weights = weights * (1.0 / jnp.sum(weights, axis=0, keepdims=True))
        low = weights.astype(BF16)
        deltas = jnp.sum(low.astype(F32) * grad_w, axis=0, keepdims=True)
        grad_s = (weights * (grad_w - deltas)).astype(BF16)
        grad_q = SCALE * lax.dot_general(grad_s, kc, TN, preferred_element_type=F32)
        for i in range(2):
            gq_ref[rows, pl.ds((2 * g + i) * HD, HD)] = grad_q[i * BLOCK : (i + 1) * BLOCK].astype(BF16)
        lines = jnp.concatenate([grad_s, low], axis=1)
        term = jnp.concatenate(
            [
                jnp.dot(lines[:HALF_K], pair, preferred_element_type=F32),
                jnp.dot(lines[HALF_K:], pair, preferred_element_type=F32),
            ],
            axis=0,
        )
        for s in range(TOPK):
            part = term[s * BLOCK : (s + 1) * BLOCK]
            tm_ref[q, s, :, :HD] = (SCALE * part[:, :HD]).astype(BF16)
            tm_ref[q, s, :, HD:] = part[:, HD:].astype(BF16)

    def terms(g, plane):
        def body(i, carry):
            for b in range(2 * CHUNK):
                j = (plane * 4 + i) * (2 * CHUNK) + b
                total = tm_ref[0, inv_ref[0, g, j]].astype(F32)
                for q in range(1, CHUNK):
                    total = total + tm_ref[q, inv_ref[q, g, j]].astype(F32)
                total = total.astype(BF16)
                lines = pl.ds((b % CHUNK) * BLOCK, BLOCK)
                t_ref[2 * g, plane, b // CHUNK, i, lines, :] = total[:, :HD]
                t_ref[2 * g + 1, plane, b // CHUNK, i, lines, :] = total[:, HD:]
            return carry

        lax.fori_loop(0, 4, body, 0)

    planes = (py, yh)
    core_sums = {
        (u, n): plan(t_ref.at[u, planes[n], 1 - k], p_ref.at[u, planes[n]], to_core)
        for u in range(4)
        for n in range(2)
    }

    class Sum:
        def __init__(self, way, theirs, mine, bufs, places, ends, over):
            self.way, self.theirs, self.mine, self.bufs = way, theirs, mine, bufs
            self.here, right, left, across = places
            self.across = across
            go_right, go_left = ends
            first, far, l0, r0, l1, r1, stage, last = bufs
            self.first = plan(theirs.at[across], first, over)
            self.theirs_right = plan(theirs.at[right], l1, go_right)
            self.theirs_left = plan(theirs.at[left], r1, go_left)
            self.far = plan(mine.at[across], far, go_right if way == 0 else go_left)
            self.mine_right = plan(mine.at[right], l0, go_right)
            self.mine_left = plan(mine.at[left], r0, go_left)
            self.relayed, self.direct = (
                (self.mine_right, self.mine_left) if way == 0 else (self.mine_left, self.mine_right)
            )
            self.relay_at = right if way == 0 else left
            self.over = plan(stage, last, over)

        def start_first(self):
            self.first.start()

        def start_near(self):
            self.theirs_right.start()
            self.theirs_left.start()

        def start_theirs(self):
            self.start_first()
            self.start_near()

        def start_mine(self):
            self.direct.start()

        def add(self, i, buf):
            self.mine[i] = (self.mine[i].astype(F32) + buf[...].astype(F32)).astype(BF16)

        def go_far(self):
            self.first.wait_recv()
            self.add(self.across, self.bufs[0])
            self.far.start()

        def cross(self):
            _, _, _, _, l1, r1, stage, _ = self.bufs
            self.theirs_right.wait_recv()
            self.theirs_left.wait_recv()
            total = self.theirs[self.here].astype(F32) + l1[...].astype(F32) + r1[...].astype(F32)
            stage[...] = total.astype(BF16)
            self.over.start()

        def relay(self):
            self.far.wait_recv()
            self.add(self.relay_at, self.bufs[1])
            self.relayed.start()

        def end(self):
            _, _, l0, r0, _, _, _, last = self.bufs
            self.mine_right.wait_recv()
            self.mine_left.wait_recv()
            total = self.mine[self.here].astype(F32) + l0[...].astype(F32) + r0[...].astype(F32)
            self.over.wait_recv()
            return total + last[...].astype(F32)

    x_sums = {
        (u, e): Sum(
            u % 2, s_ref.at[u, e, py], s_ref.at[u, e, yh],
            (xa_ref.at[u, e], xf_ref.at[u, e], xl_ref.at[u, e, 0], xr_ref.at[u, e, 0],
             xl_ref.at[u, e, 1], xr_ref.at[u, e, 1], xs_ref.at[u, e], xy_ref.at[u, e]),
            (x, xr, xl, xo), (to_right, to_left), to_y,
        )
        for u in range(4)
        for e in range(2)
    }

    def core_sum(u, n):
        plane = planes[n]
        core_sums[u, n].wait_recv()
        for e in range(2):
            half = pl.ds(e * HD, HD)
            for xx in range(4):
                s_ref[u, e, plane, xx] = (
                    t_ref[u, plane, k, xx, half, :].astype(F32) + p_ref[u, plane, xx, half, :].astype(F32)
                ).astype(BF16)

    def sum_end(u, e):
        g, kv = units[u]
        (gk_ref, gv_ref)[kv][pl.ds(e * HD, HD), pl.ds(g * HD, HD)] = x_sums[u, e].end().astype(BF16)

    def do(names, *steps):
        for step in steps:
            for name in names:
                getattr(x_sums[name], step)()

    def core_start(g, n):
        core_sums[2 * g, n].start()
        core_sums[2 * g + 1, n].start()

    LOW = [[(0, e), (1, e)] for e in range(2)]
    HIGH = [[(2, e), (3, e)] for e in range(2)]
    hooks = {
        (0, 1): lambda: (
            each(gather_relay, (2, 1), (3, 1)),
            each(gather_far, (2, 1), (3, 1)),
        ),
        (1, 1): lambda: (
            each(core_sum, (0, 0), (1, 0)),
            do(LOW[0] + LOW[1], "start_theirs"),
            each(core_sum, (0, 1), (1, 1)),
            do(LOW[0] + LOW[1], "start_mine"),
        ),
    }
    for g in range(2):
        if g == 1:
            each(gather_end, (2,), (3,))

        def step(q, carry, g=g):
            for (gg, at), action in hooks.items():
                if gg == g:
                    pl.when(q == at)(lambda action=action: (action(), None)[1])
            attend(g, 2 * q)
            attend(g, 2 * q + 1)
            return carry

        lax.fori_loop(0, CHUNK // 2, step, 0)
        if g == 1:
            out_copies.append(local(gq_ref, gq_hbm))
        for n in range(2):
            terms(g, planes[n])
            core_start(g, n)
    do(LOW[0] + LOW[1], "go_far")

    for copy in weight_copies:
        copy.wait()

    def query_part(i, carry):
        rows = pl.ds(pl.multiple_of(i * OUT_W, OUT_W), OUT_W)
        acc_ref[rows, :] = lax.dot_general(wq_ref[rows, :], gq_ref[...], NT, preferred_element_type=F32)
        return carry

    each(core_sum, (2, 0), (3, 0))
    do(HIGH[0], "start_theirs")
    do(HIGH[1], "start_first")
    each(core_sum, (2, 1), (3, 1))
    do(LOW[0], "cross")
    lax.fori_loop(0, 4, query_part, 0)
    do(LOW[0] + LOW[1], "relay")
    lax.fori_loop(4, 5, query_part, 0)
    do(HIGH[0], "go_far", "start_mine", "cross")
    do(LOW[1], "cross")
    do(HIGH[1][:1], "start_near")
    lax.fori_loop(5, 8, query_part, 0)
    do(HIGH[0], "relay")
    do(HIGH[1][1:], "start_near")
    do(HIGH[1], "go_far", "start_mine")
    each(sum_end, *((u, 0) for u in range(4)))

    z_places = (z, zr, zl, zo)
    z_sums = {
        (e, w): Sum(
            w, pt_ref.at[e, w, 1 - yl], pt_ref.at[e, w, yl],
            (za_ref.at[e, w], zf_ref.at[e, w], zl_ref.at[e, w, 0], zr_ref.at[e, w, 0],
             zl_ref.at[e, w, 1], zr_ref.at[e, w, 1], zs_ref.at[e, w], zy_ref.at[e, w]),
            z_places, (to_zr, to_zl), to_yl,
        )
        for e in range(2)
        for w in range(2)
    }

    def term_chunk(e, side, zz):
        i = zz * 2 + side
        rows = pl.ds(pl.multiple_of(i * OUT_W, OUT_W), OUT_W)
        half = pl.ds(e * HD, HD)
        out = acc_ref[rows, half]
        out = out + lax.dot_general(wk_ref[rows, :], gk_ref[half, :], NT, preferred_element_type=F32)
        out = out + lax.dot_general(wv_ref[rows, :], gv_ref[half, :], NT, preferred_element_type=F32)
        out = out.astype(BF16)
        for w in range(2):
            pt_ref[e, w, side, zz] = out[w * HALF_W : (w + 1) * HALF_W]

    def both(e, step):
        for w in range(2):
            step(z_sums[e, w])

    def send_first(e):
        term_chunk(e, 1 - yl, zo)
        both(e, lambda t: t.first.start())

    def send_near(e):
        term_chunk(e, 1 - yl, zr)
        both(e, lambda t: t.theirs_right.start())
        term_chunk(e, 1 - yl, zl)
        both(e, lambda t: t.theirs_left.start())

    def own_chunks(e):
        for zz in (zo, zl, zr):
            term_chunk(e, yl, zz)

    def last_chunks(e):
        term_chunk(e, 1 - yl, z)
        term_chunk(e, yl, z)

    def z_end(e):
        for w in range(2):
            gi_ref[pl.ds(w * HALF_W, HALF_W), pl.ds(e * HD, HD)] = z_sums[e, w].end().astype(BF16)

    send_first(0)
    do(HIGH[1], "relay")
    send_near(0)
    do(HIGH[1], "cross")
    own_chunks(0)
    last_chunks(0)
    both(0, lambda t: (t.go_far(), t.start_mine()))
    each(sum_end, *((u, 1) for u in range(4)))
    out_copies.append(local(gk_ref, gk_hbm))
    out_copies.append(local(gv_ref, gv_hbm))
    send_first(1)
    send_near(1)
    own_chunks(1)
    last_chunks(1)
    both(0, lambda t: t.cross())
    both(1, lambda t: (t.go_far(), t.start_mine()))
    both(0, lambda t: t.relay())
    both(1, lambda t: t.cross())
    both(1, lambda t: t.relay())
    z_end(0)
    z_end(1)
    out_copies.append(local(gi_ref, gi_hbm))

    for copy in out_copies:
        copy.wait()
    for copy in started:
        copy.wait_send()


def write_out(*refs):
    sources, targets, held, sem = refs[:4], refs[4:8], refs[8:12], refs[12]
    loads = [pltpu.make_async_copy(sources[i], held[i], sem.at[i]) for i in range(4)]
    stores = [pltpu.make_async_copy(held[i], targets[i], sem.at[4 + i]) for i in range(4)]
    for copy in loads:
        copy.start()
    for load, store in zip(loads, stores):
        load.wait()
        store.start()
    for copy in stores:
        copy.wait()


def body(queries, keys, values, grad_out, chosen, w_query, w_key, w_value):
    hbm = pl.BlockSpec(memory_space=pl.ANY)
    shape = jax.ShapeDtypeStruct
    buf = lambda *dims: pltpu.VMEM(dims, BF16)
    chunk = (ROWS, HD)
    zc = (2, HALF_W, HD)
    outs = pl.pallas_call(
        kernel,
        out_shape=(
            shape((ROWS, 512), BF16),
            shape((ROWS, 256), BF16),
            shape((ROWS, 256), BF16),
            shape((OUT_W, ROWS), BF16),
        ),
        in_specs=[hbm] * 8,
        out_specs=(hbm,) * 4,
        scratch_shapes=[
            buf(64, BLOCK, HD), buf(64, BLOCK, HD), buf(64, BLOCK, HD), buf(64, BLOCK, HD),
            buf(ROWS, 512), buf(ROWS, 512), buf(ROWS, 512), buf(ROWS, 256), buf(ROWS, 256), buf(OUT_W, ROWS),
            buf(CHUNK, TOPK + 1, BLOCK, 2 * HD),
            pltpu.SMEM((CHUNK, 2, TOPK), jnp.int32), pltpu.VMEM((CHUNK, 2, TOPK), jnp.int32),
            pltpu.VMEM((CHUNK, 2, HD), jnp.int32), pltpu.SMEM((CHUNK, 2, HD), jnp.int32),
            buf(4, 2, 2, 4, *chunk), buf(4, 2, 4, *chunk), buf(4, 2, 2, 4, HD, HD),
            buf(4, 2, HD, HD), buf(4, 2, HD, HD), buf(4, 2, 2, HD, HD), buf(4, 2, 2, HD, HD), buf(4, 2, HD, HD), buf(4, 2, HD, HD),
            buf(4608, 512), buf(4608, 256), buf(4608, 256), pltpu.VMEM((4608, ROWS), F32),
            buf(2, 2, 2, 4, HALF_W, HD), buf(2, *zc), buf(2, *zc),
            buf(2, 2, 2, HALF_W, HD), buf(2, 2, 2, HALF_W, HD), buf(2, *zc), buf(2, *zc),
            pltpu.SemaphoreType.DMA((N_COPIES,)),
            pltpu.SemaphoreType.DMA((N_COPIES,)),
            pltpu.SemaphoreType.DMA((32,)),
        ],
        compiler_params=pltpu.CompilerParams(
            collective_id=0, has_side_effects=True, vmem_limit_bytes=60 * 1024 * 1024
        ),
    )(queries, grad_out, keys, values, chosen, w_query, w_key, w_value)
    grad_queries, grad_keys, grad_values, grad_input = pl.pallas_call(
        write_out,
        out_shape=tuple(shape(o.shape, o.dtype) for o in outs),
        in_specs=[hbm] * 4,
        out_specs=(hbm,) * 4,
        scratch_shapes=[pltpu.VMEM(o.shape, o.dtype) for o in outs] + [pltpu.SemaphoreType.DMA((8,))],
        compiler_params=pltpu.CompilerParams(vmem_limit_bytes=60 * 1024 * 1024),
    )(*outs)
    return grad_queries, grad_keys, grad_values, grad_input.T


def solution(mesh):
    both = P("ctx", "head")
    return jax.shard_map(
        body,
        mesh=mesh,
        in_specs=(both, both, both, both, P("ctx", "head", None)) + (P(None, "head"),) * 3,
        out_specs=(both, both, both, both),
        check_vma=False,
    )
```

```python
import functools
import math

import jax
import jax.numpy as jnp
from jax import lax
from jax.experimental import pallas as pl
from jax.experimental.pallas import tpu as pltpu
from jax.sharding import PartitionSpec as P

HD = 128
BLOCK = 64
TOPK = 16
NX = 4
ROWS = 256
CHUNK = 4
OUT_W = 576
HALF_W = OUT_W // 2
HALF_K = TOPK * BLOCK // 2
SCALE = 1.0 / math.sqrt(HD)
EXP2_SCALE = SCALE / math.log(2.0)
NT = (((1,), (1,)), ((), ()))
TN = (((0,), (0,)), ((), ()))
F32 = jnp.float32
BF16 = jnp.bfloat16
N_COPIES = 184


def kernel(
    q_hbm, go_hbm, k_hbm, v_hbm, ch_hbm, wq_hbm, wk_hbm, wv_hbm,
    gq_hbm, gk_hbm, gv_hbm, gi_hbm,
    kv00, kv01, kv10, kv11, q_ref, go_ref, gq_ref, gk_ref, gv_ref, gi_ref,
    tm_ref, ch_ref, chv_ref, names_ref, inv_ref,
    t_ref, p_ref, s_ref, xa_ref, xf_ref, xl_ref, xr_ref, xs_ref, xy_ref,
    wq_ref, wk_ref, wv_ref, acc_ref, pt_ref, za_ref, zf_ref, zl_ref, zr_ref, zs_ref, zy_ref,
    send_sem, recv_sem, local_sem,
):
    c = lax.axis_index("ctx")
    h = lax.axis_index("head")
    yh, x, k = c // 8, (c // 2) % 4, c % 2
    z, yl = h // 2, h % 2
    kv_bufs = ((kv00, kv01), (kv10, kv11))

    def ctx_at(p, xx, kk):
        return p * 8 + xx * 2 + kk

    xr, xl, xo = (x + 1) % 4, (x + 3) % 4, (x + 2) % 4
    zr, zl, zo = (z + 1) % 4, (z + 3) % 4, (z + 2) % 4
    py = 1 - yh
    to_right = (ctx_at(yh, xr, k), h)
    to_left = (ctx_at(yh, xl, k), h)
    to_y = (ctx_at(py, x, k), h)
    to_core = (ctx_at(yh, x, 1 - k), h)
    to_zr = (c, zr * 2 + yl)
    to_zl = (c, zl * 2 + yl)
    to_yl = (c, z * 2 + (1 - yl))

    started = []
    one_way = set()

    def plan(src, dst, where):
        i = len(started)
        copy = pltpu.make_async_remote_copy(
            src_ref=src,
            dst_ref=dst,
            send_sem=send_sem.at[i],
            recv_sem=recv_sem.at[i],
            device_id=where,
            device_id_type=pl.DeviceIdType.MESH,
        )
        started.append(copy)
        return copy

    def send(src, dst, where):
        copy = plan(src, dst, where)
        copy.start()
        return copy

    barrier = pltpu.get_barrier_semaphore()
    partners = (to_right, to_left, to_y, to_core, to_zr, to_zl, to_yl)
    for where in partners:
        pl.semaphore_signal(barrier, inc=1, device_id=where, device_id_type=pl.DeviceIdType.MESH)

    own_copies = []
    choice_copies = [
        pltpu.make_async_copy(ch_hbm, chv_ref, local_sem.at[30]),
        pltpu.make_async_copy(ch_hbm, ch_ref, local_sem.at[31]),
    ]
    for copy in choice_copies:
        copy.start()
    n_local = 0
    for g in range(2):
        for kv in range(2):
            src = (k_hbm, v_hbm)[kv]
            group = []
            for b in range(CHUNK):
                copy = pltpu.make_async_copy(
                    src.at[pl.ds(b * BLOCK, BLOCK), pl.ds(g * HD, HD)],
                    kv_bufs[g][kv].at[c * CHUNK + b],
                    local_sem.at[n_local],
                )
                n_local += 1
                copy.start()
                group.append(copy)
            own_copies.append(group)

    def local(src, dst):
        nonlocal n_local
        copy = pltpu.make_async_copy(src, dst, local_sem.at[n_local])
        n_local += 1
        copy.start()
        return copy

    query_copies = [local(q_hbm, q_ref), local(go_hbm, go_ref)]
    weight_copies = [local(wq_hbm, wq_ref), local(wk_hbm, wk_ref), local(wv_hbm, wv_ref)]
    out_copies = []

    for copy in choice_copies:
        copy.wait()
    lanes = lax.broadcasted_iota(jnp.int32, (2, HD), 1)
    for q in range(CHUNK):
        picked = chv_ref[q]
        found = jnp.full((2, HD), TOPK, jnp.int32)
        for n in range(TOPK):
            found = jnp.where(picked[:, n : n + 1] == lanes, n, found)
        names_ref[q] = found
        tm_ref[q, TOPK] = jnp.zeros((BLOCK, 2 * HD), BF16)

    pl.semaphore_wait(barrier, len(partners))
    names_copy = local(names_ref, inv_ref)

    units = [(g, kv) for g in range(2) for kv in range(2)]

    def slot(u, idx):
        g, kv = units[u]
        return kv_bufs[g][kv].at[pl.ds(pl.multiple_of(idx * CHUNK, CHUNK), CHUNK)]

    def put(u, idx, where):
        return plan(slot(u, idx), slot(u, idx), where)

    g_near, g_far, g_core, g_y = {}, {}, {}, {}
    for u in range(4):
        g_y[u] = put(u, c, to_y)
        for n, plane in enumerate((yh, py)):
            first = ctx_at(plane, x, k)
            g_near[u, n] = (put(u, first, to_right), put(u, first, to_left))
            if n == 1:
                g_far[u, n] = put(u, ctx_at(yh, xo, k), to_y)
            elif units[u][1] == 0:
                g_far[u, n] = put(u, ctx_at(plane, xl, k), to_right)
            else:
                g_far[u, n] = put(u, ctx_at(plane, xr, k), to_left)
            g_core[u, n] = [put(u, ctx_at(plane, xx, k), to_core) for xx in (x, xl, xr, xo)]

    def gather_first(u):
        for copy in own_copies[u]:
            copy.wait()
        g_near[u, 0][0].start()
        g_near[u, 0][1].start()
        g_core[u, 0][0].start()

    def gather_over(u):
        g_y[u].start()

    def gather_relay(u, n):
        for side in range(2):
            g_near[u, n][side].wait_recv()
            if n == 0 and units[u][1] == side:
                g_far[u, 0].start()
            g_core[u, n][1 + side].start()

    def gather_y(u):
        g_y[u].wait_recv()
        g_near[u, 1][0].start()
        g_near[u, 1][1].start()
        g_core[u, 1][0].start()

    def gather_far(u, n):
        g_far[u, n].wait_recv()
        if n == 0:
            g_far[u, 1].start()
        g_core[u, n][3].start()

    def gather_end(u):
        for n in range(2):
            for copy in g_core[u, n]:
                copy.wait_recv()

    def each(step, *names):
        for name in names:
            step(*name)

    for u in range(4):
        gather_first(u)
        gather_over(u)
    each(gather_relay, *((u, 0) for u in range(4)))
    each(gather_y, *((u,) for u in range(4)))
    each(gather_far, *((u, 0) for u in range(4)))
    each(gather_relay, (0, 1), (1, 1))
    each(gather_far, (0, 1), (1, 1))
    each(gather_end, (0,), (1,))
    for copy in query_copies:
        copy.wait()
    names_copy.wait()

    base = lax.broadcasted_iota(jnp.int32, (BLOCK, HD), 0) - (
        lax.broadcasted_iota(jnp.int32, (BLOCK, HD), 1) % BLOCK
    )

    def attend(g, q):
        own = c * CHUNK + q
        rows = pl.ds(pl.multiple_of(q * BLOCK, BLOCK), BLOCK)
        qb = jnp.concatenate([q_ref[rows, pl.ds((2 * g + i) * HD, HD)] for i in range(2)], axis=0)
        gb = jnp.concatenate([go_ref[rows, pl.ds((2 * g + i) * HD, HD)] for i in range(2)], axis=0)
        none = jnp.zeros((HD, HD), BF16)
        pair = jnp.concatenate(
            [jnp.concatenate([qb, none], axis=1), jnp.concatenate([none, gb], axis=1)], axis=0
        )
        blocks = [ch_ref[q, g, s] for s in range(TOPK)]
        kc = jnp.concatenate([kv_bufs[g][0][b] for b in blocks], axis=0)
        vc = jnp.concatenate([kv_bufs[g][1][b] for b in blocks], axis=0)
        lines = jnp.concatenate([kc, vc], axis=1)
        products = jnp.concatenate(
            [
                lax.dot_general(lines[:HALF_K], pair, NT, preferred_element_type=F32),
                lax.dot_general(lines[HALF_K:], pair, NT, preferred_element_type=F32),
            ],
            axis=0,
        )
        grad_w = products[:, HD:]
        scores = jnp.concatenate(
            [
                jnp.where(
                    base <= (own - blocks[s]) * BLOCK,
                    products[s * BLOCK : (s + 1) * BLOCK, :HD],
                    -1e30,
                )
                for s in range(TOPK)
            ],
            axis=0,
        )
        top = jnp.max(scores, axis=0, keepdims=True)
        weights = jnp.exp2((scores - top) * EXP2_SCALE)
        weights = weights * (1.0 / jnp.sum(weights, axis=0, keepdims=True))
        low = weights.astype(BF16)
        deltas = jnp.sum(low.astype(F32) * grad_w, axis=0, keepdims=True)
        grad_s = (weights * (grad_w - deltas)).astype(BF16)
        grad_q = SCALE * lax.dot_general(grad_s, kc, TN, preferred_element_type=F32)
        for i in range(2):
            gq_ref[rows, pl.ds((2 * g + i) * HD, HD)] = grad_q[i * BLOCK : (i + 1) * BLOCK].astype(BF16)
        lines = jnp.concatenate([grad_s, low], axis=1)
        term = jnp.concatenate(
            [
                jnp.dot(lines[:HALF_K], pair, preferred_element_type=F32),
                jnp.dot(lines[HALF_K:], pair, preferred_element_type=F32),
            ],
            axis=0,
        )
        for s in range(TOPK):
            part = term[s * BLOCK : (s + 1) * BLOCK]
            tm_ref[q, s, :, :HD] = (SCALE * part[:, :HD]).astype(BF16)
            tm_ref[q, s, :, HD:] = part[:, HD:].astype(BF16)

    def terms(g, plane):
        def body(i, carry):
            for b in range(2 * CHUNK):
                j = (plane * 4 + i) * (2 * CHUNK) + b
                total = tm_ref[0, inv_ref[0, g, j]].astype(F32)
                for q in range(1, CHUNK):
                    total = total + tm_ref[q, inv_ref[q, g, j]].astype(F32)
                total = total.astype(BF16)
                lines = pl.ds((b % CHUNK) * BLOCK, BLOCK)
                t_ref[2 * g, plane, b // CHUNK, i, lines, :] = total[:, :HD]
                t_ref[2 * g + 1, plane, b // CHUNK, i, lines, :] = total[:, HD:]
            return carry

        lax.fori_loop(0, 4, body, 0)

    planes = (py, yh)
    core_sums = {
        (u, n): plan(t_ref.at[u, planes[n], 1 - k], p_ref.at[u, planes[n]], to_core)
        for u in range(4)
        for n in range(2)
    }

    class Sum:
        def __init__(self, way, theirs, mine, bufs, places, ends, over, sender=None):
            self.sender = sender
            begin = len(started)
            self.way, self.theirs, self.mine, self.bufs = way, theirs, mine, bufs
            self.here, right, left, across = places
            self.across = across
            go_right, go_left = ends
            first, far, l0, r0, l1, r1, stage, last = bufs
            self.first = plan(theirs.at[across], first, over)
            self.theirs_right = plan(theirs.at[right], l1, go_right)
            self.theirs_left = plan(theirs.at[left], r1, go_left)
            self.over = plan(stage, last, over)
            if sender is not None:
                one_way.update(range(begin, len(started)))
            self.far = plan(mine.at[across], far, go_right if way == 0 else go_left)
            self.mine_right = plan(mine.at[right], l0, go_right)
            self.mine_left = plan(mine.at[left], r0, go_left)
            self.relayed, self.direct = (
                (self.mine_right, self.mine_left) if way == 0 else (self.mine_left, self.mine_right)
            )
            self.relay_at = right if way == 0 else left

        def gate(self, sends, action):
            if self.sender is None:
                action()
            else:
                pl.when(self.sender if sends else jnp.logical_not(self.sender))(action)

        def start_first(self):
            self.gate(True, self.first.start)

        def start_near(self):
            def action():
                self.theirs_right.start()
                self.theirs_left.start()

            self.gate(True, action)

        def start_theirs(self):
            self.start_first()
            self.start_near()

        def start_mine(self):
            self.direct.start()

        def add(self, i, buf):
            self.mine[i] = (self.mine[i].astype(F32) + buf[...].astype(F32)).astype(BF16)

        def far_now(self):
            self.gate(True, self.far.start)

        def go_far(self):
            def action():
                self.first.wait_recv()
                self.add(self.across, self.bufs[0])
                self.far.start()

            self.gate(False, action)

        def cross(self):
            def action():
                _, _, _, _, l1, r1, stage, _ = self.bufs
                self.theirs_right.wait_recv()
                self.theirs_left.wait_recv()
                total = self.theirs[self.here].astype(F32) + l1[...].astype(F32) + r1[...].astype(F32)
                stage[...] = total.astype(BF16)
                self.over.start()

            self.gate(True, action)

        def relay(self):
            self.far.wait_recv()
            self.add(self.relay_at, self.bufs[1])
            self.relayed.start()

        def end(self):
            _, _, l0, r0, _, _, _, last = self.bufs
            self.mine_right.wait_recv()
            self.mine_left.wait_recv()
            total = self.mine[self.here].astype(F32) + l0[...].astype(F32) + r0[...].astype(F32)
            self.gate(False, self.over.wait_recv)
            return total + last[...].astype(F32)

    later = yh == 1

    @pl.when(later)
    def _():
        xy_ref[...] = jnp.zeros(xy_ref.shape, BF16)

    x_sums = {
        (u, e): Sum(
            u % 2, s_ref.at[u, e, py], s_ref.at[u, e, yh],
            (xa_ref.at[u, e], xf_ref.at[u, e], xl_ref.at[u, e, 0], xr_ref.at[u, e, 0],
             xl_ref.at[u, e, 1], xr_ref.at[u, e, 1], xs_ref.at[u, e], xy_ref.at[u, e]),
            (x, xr, xl, xo), (to_right, to_left), to_y, later,
        )
        for u in range(4)
        for e in range(2)
    }

    def core_sum(u, n):
        plane = planes[n]
        core_sums[u, n].wait_recv()
        for e in range(2):
            half = pl.ds(e * HD, HD)
            for xx in range(4):
                s_ref[u, e, plane, xx] = (
                    t_ref[u, plane, k, xx, half, :].astype(F32) + p_ref[u, plane, xx, half, :].astype(F32)
                ).astype(BF16)

    def sum_end(u, e):
        g, kv = units[u]
        (gk_ref, gv_ref)[kv][pl.ds(e * HD, HD), pl.ds(g * HD, HD)] = x_sums[u, e].end().astype(BF16)

    def do(names, *steps):
        for step in steps:
            for name in names:
                getattr(x_sums[name], step)()

    def core_start(g, n):
        core_sums[2 * g, n].start()
        core_sums[2 * g + 1, n].start()

    LOW = [[(0, e), (1, e)] for e in range(2)]
    HIGH = [[(2, e), (3, e)] for e in range(2)]
    hooks = {
        (0, 1): lambda: (
            each(gather_relay, (2, 1), (3, 1)),
            each(gather_far, (2, 1), (3, 1)),
        ),
        (1, 1): lambda: (
            each(core_sum, (0, 0), (1, 0)),
            do(LOW[0] + LOW[1], "start_theirs"),
            each(core_sum, (0, 1), (1, 1)),
            do(LOW[0] + LOW[1], "far_now", "start_mine"),
        ),
    }
    for g in range(2):
        if g == 1:
            each(gather_end, (2,), (3,))

        def step(q, carry, g=g):
            for (gg, at), action in hooks.items():
                if gg == g:
                    pl.when(q == at)(lambda action=action: (action(), None)[1])
            attend(g, 2 * q)
            attend(g, 2 * q + 1)
            return carry

        lax.fori_loop(0, CHUNK // 2, step, 0)
        if g == 1:
            out_copies.append(local(gq_ref, gq_hbm))
        for n in range(2):
            terms(g, planes[n])
            core_start(g, n)
    do(LOW[0] + LOW[1], "go_far")

    for copy in weight_copies:
        copy.wait()

    def query_part(i, carry):
        rows = pl.ds(pl.multiple_of(i * OUT_W, OUT_W), OUT_W)
        acc_ref[rows, :] = lax.dot_general(wq_ref[rows, :], gq_ref[...], NT, preferred_element_type=F32)
        return carry

    each(core_sum, (2, 0), (3, 0))
    do(HIGH[0], "start_theirs")
    do(HIGH[1], "start_first")
    each(core_sum, (2, 1), (3, 1))
    do(HIGH[0], "far_now")
    do(LOW[0], "cross")
    lax.fori_loop(0, 4, query_part, 0)
    do(HIGH[0], "go_far")
    do(LOW[0] + LOW[1], "relay")
    lax.fori_loop(4, 5, query_part, 0)
    do(HIGH[0], "start_mine", "cross")
    do(LOW[1], "cross")
    do(HIGH[1][:1], "start_near")
    lax.fori_loop(5, 8, query_part, 0)
    do(HIGH[0], "relay")
    do(HIGH[1][1:], "start_near")
    do(HIGH[1], "far_now", "go_far", "start_mine")
    each(sum_end, *((u, 0) for u in range(4)))

    z_places = (z, zr, zl, zo)
    z_sums = {
        (e, w): Sum(
            w, pt_ref.at[e, w, 1 - yl], pt_ref.at[e, w, yl],
            (za_ref.at[e, w], zf_ref.at[e, w], zl_ref.at[e, w, 0], zr_ref.at[e, w, 0],
             zl_ref.at[e, w, 1], zr_ref.at[e, w, 1], zs_ref.at[e, w], zy_ref.at[e, w]),
            z_places, (to_zr, to_zl), to_yl,
        )
        for e in range(2)
        for w in range(2)
    }

    def term_chunk(e, side, zz):
        i = zz * 2 + side
        rows = pl.ds(pl.multiple_of(i * OUT_W, OUT_W), OUT_W)
        half = pl.ds(e * HD, HD)
        out = acc_ref[rows, half]
        out = out + lax.dot_general(wk_ref[rows, :], gk_ref[half, :], NT, preferred_element_type=F32)
        out = out + lax.dot_general(wv_ref[rows, :], gv_ref[half, :], NT, preferred_element_type=F32)
        out = out.astype(BF16)
        for w in range(2):
            pt_ref[e, w, side, zz] = out[w * HALF_W : (w + 1) * HALF_W]

    def both(e, step):
        for w in range(2):
            step(z_sums[e, w])

    def send_first(e):
        term_chunk(e, 1 - yl, zo)
        both(e, lambda t: t.first.start())

    def send_near(e):
        term_chunk(e, 1 - yl, zr)
        both(e, lambda t: t.theirs_right.start())
        term_chunk(e, 1 - yl, zl)
        both(e, lambda t: t.theirs_left.start())

    def own_chunks(e):
        for zz in (zo, zl, zr):
            term_chunk(e, yl, zz)

    def last_chunks(e):
        term_chunk(e, 1 - yl, z)
        term_chunk(e, yl, z)

    def z_end(e):
        for w in range(2):
            gi_ref[pl.ds(w * HALF_W, HALF_W), pl.ds(e * HD, HD)] = z_sums[e, w].end().astype(BF16)

    do(HIGH[1], "cross")
    send_first(0)
    do(HIGH[1], "relay")
    send_near(0)
    own_chunks(0)
    last_chunks(0)
    both(0, lambda t: (t.go_far(), t.start_mine()))
    each(sum_end, *((u, 1) for u in range(4)))
    out_copies.append(local(gk_ref, gk_hbm))
    out_copies.append(local(gv_ref, gv_hbm))
    send_first(1)
    send_near(1)
    own_chunks(1)
    last_chunks(1)
    both(0, lambda t: t.cross())
    both(1, lambda t: (t.go_far(), t.start_mine()))
    both(0, lambda t: t.relay())
    both(1, lambda t: t.cross())
    both(1, lambda t: t.relay())
    z_end(0)
    z_end(1)
    out_copies.append(local(gi_ref, gi_hbm))

    for copy in out_copies:
        copy.wait()
    for i, copy in enumerate(started):
        if i in one_way:
            pl.when(later)(copy.wait_send)
        else:
            copy.wait_send()


def write_out(*refs):
    sources, targets, held, sem = refs[:4], refs[4:8], refs[8:12], refs[12]
    loads = [pltpu.make_async_copy(sources[i], held[i], sem.at[i]) for i in range(4)]
    stores = [pltpu.make_async_copy(held[i], targets[i], sem.at[4 + i]) for i in range(4)]
    for copy in loads:
        copy.start()
    for load, store in zip(loads, stores):
        load.wait()
        store.start()
    for copy in stores:
        copy.wait()


def body(queries, keys, values, grad_out, chosen, w_query, w_key, w_value):
    hbm = pl.BlockSpec(memory_space=pl.ANY)
    shape = jax.ShapeDtypeStruct
    buf = lambda *dims: pltpu.VMEM(dims, BF16)
    chunk = (ROWS, HD)
    zc = (2, HALF_W, HD)
    outs = pl.pallas_call(
        kernel,
        out_shape=(
            shape((ROWS, 512), BF16),
            shape((ROWS, 256), BF16),
            shape((ROWS, 256), BF16),
            shape((OUT_W, ROWS), BF16),
        ),
        in_specs=[hbm] * 8,
        out_specs=(hbm,) * 4,
        scratch_shapes=[
            buf(64, BLOCK, HD), buf(64, BLOCK, HD), buf(64, BLOCK, HD), buf(64, BLOCK, HD),
            buf(ROWS, 512), buf(ROWS, 512), buf(ROWS, 512), buf(ROWS, 256), buf(ROWS, 256), buf(OUT_W, ROWS),
            buf(CHUNK, TOPK + 1, BLOCK, 2 * HD),
            pltpu.SMEM((CHUNK, 2, TOPK), jnp.int32), pltpu.VMEM((CHUNK, 2, TOPK), jnp.int32),
            pltpu.VMEM((CHUNK, 2, HD), jnp.int32), pltpu.SMEM((CHUNK, 2, HD), jnp.int32),
            buf(4, 2, 2, 4, *chunk), buf(4, 2, 4, *chunk), buf(4, 2, 2, 4, HD, HD),
            buf(4, 2, HD, HD), buf(4, 2, HD, HD), buf(4, 2, 2, HD, HD), buf(4, 2, 2, HD, HD), buf(4, 2, HD, HD), buf(4, 2, HD, HD),
            buf(4608, 512), buf(4608, 256), buf(4608, 256), pltpu.VMEM((4608, ROWS), F32),
            buf(2, 2, 2, 4, HALF_W, HD), buf(2, *zc), buf(2, *zc),
            buf(2, 2, 2, HALF_W, HD), buf(2, 2, 2, HALF_W, HD), buf(2, *zc), buf(2, *zc),
            pltpu.SemaphoreType.DMA((N_COPIES,)),
            pltpu.SemaphoreType.DMA((N_COPIES,)),
            pltpu.SemaphoreType.DMA((32,)),
        ],
        compiler_params=pltpu.CompilerParams(
            collective_id=0, has_side_effects=True, vmem_limit_bytes=60 * 1024 * 1024
        ),
    )(queries, grad_out, keys, values, chosen, w_query, w_key, w_value)
    grad_queries, grad_keys, grad_values, grad_input = pl.pallas_call(
        write_out,
        out_shape=tuple(shape(o.shape, o.dtype) for o in outs),
        in_specs=[hbm] * 4,
        out_specs=(hbm,) * 4,
        scratch_shapes=[pltpu.VMEM(o.shape, o.dtype) for o in outs] + [pltpu.SemaphoreType.DMA((8,))],
        compiler_params=pltpu.CompilerParams(vmem_limit_bytes=60 * 1024 * 1024),
    )(*outs)
    return grad_queries, grad_keys, grad_values, grad_input.T


def solution(mesh):
    both = P("ctx", "head")
    return jax.shard_map(
        body,
        mesh=mesh,
        in_specs=(both, both, both, both, P("ctx", "head", None)) + (P(None, "head"),) * 3,
        out_specs=(both, both, both, both),
        check_vma=False,
    )
```

```python
import functools
import math

import jax
import jax.numpy as jnp
from jax import lax
from jax.experimental import pallas as pl
from jax.experimental.pallas import tpu as pltpu
from jax.sharding import PartitionSpec as P

HD = 128
BLOCK = 64
TOPK = 16
NX = 4
ROWS = 256
CHUNK = 4
OUT_W = 576
HALF_W = OUT_W // 2
HALF_K = TOPK * BLOCK // 2
SCALE = 1.0 / math.sqrt(HD)
EXP2_SCALE = SCALE / math.log(2.0)
NT = (((1,), (1,)), ((), ()))
TN = (((0,), (0,)), ((), ()))
F32 = jnp.float32
BF16 = jnp.bfloat16
N_COPIES = 184


def kernel(
    q_hbm, go_hbm, k_hbm, v_hbm, ch_hbm, wq_hbm, wk_hbm, wv_hbm,
    gq_hbm, gk_hbm, gv_hbm, gi_hbm,
    kv00, kv01, kv10, kv11, q_ref, go_ref, gq_ref, gk_ref, gv_ref, gi_ref,
    tm_ref, ch_ref, chv_ref, names_ref, inv_ref,
    t_ref, p_ref, s_ref, xa_ref, xf_ref, xl_ref, xr_ref, xs_ref, xy_ref,
    wq_ref, wk_ref, wv_ref, acc_ref, pt_ref, za_ref, zf_ref, zl_ref, zr_ref, zs_ref, zy_ref,
    send_sem, recv_sem, local_sem,
):
    c = lax.axis_index("ctx")
    h = lax.axis_index("head")
    yh, x, k = c // 8, (c // 2) % 4, c % 2
    z, yl = h // 2, h % 2
    kv_bufs = ((kv00, kv01), (kv10, kv11))

    def ctx_at(p, xx, kk):
        return p * 8 + xx * 2 + kk

    xr, xl, xo = (x + 1) % 4, (x + 3) % 4, (x + 2) % 4
    zr, zl, zo = (z + 1) % 4, (z + 3) % 4, (z + 2) % 4
    py = 1 - yh
    to_right = (ctx_at(yh, xr, k), h)
    to_left = (ctx_at(yh, xl, k), h)
    to_y = (ctx_at(py, x, k), h)
    to_core = (ctx_at(yh, x, 1 - k), h)
    to_zr = (c, zr * 2 + yl)
    to_zl = (c, zl * 2 + yl)
    to_yl = (c, z * 2 + (1 - yl))

    started = []
    one_way = set()

    def plan(src, dst, where):
        i = len(started)
        copy = pltpu.make_async_remote_copy(
            src_ref=src,
            dst_ref=dst,
            send_sem=send_sem.at[i],
            recv_sem=recv_sem.at[i],
            device_id=where,
            device_id_type=pl.DeviceIdType.MESH,
        )
        started.append(copy)
        return copy

    def send(src, dst, where):
        copy = plan(src, dst, where)
        copy.start()
        return copy

    barrier = pltpu.get_barrier_semaphore()
    partners = (to_right, to_left, to_y, to_core, to_zr, to_zl, to_yl)
    for where in partners:
        pl.semaphore_signal(barrier, inc=1, device_id=where, device_id_type=pl.DeviceIdType.MESH)

    own_copies = []
    choice_copies = [
        pltpu.make_async_copy(ch_hbm, chv_ref, local_sem.at[30]),
        pltpu.make_async_copy(ch_hbm, ch_ref, local_sem.at[31]),
    ]
    for copy in choice_copies:
        copy.start()
    n_local = 0
    for g in range(2):
        for kv in range(2):
            src = (k_hbm, v_hbm)[kv]
            group = []
            for b in range(CHUNK):
                copy = pltpu.make_async_copy(
                    src.at[pl.ds(b * BLOCK, BLOCK), pl.ds(g * HD, HD)],
                    kv_bufs[g][kv].at[c * CHUNK + b],
                    local_sem.at[n_local],
                )
                n_local += 1
                copy.start()
                group.append(copy)
            own_copies.append(group)

    def local(src, dst):
        nonlocal n_local
        copy = pltpu.make_async_copy(src, dst, local_sem.at[n_local])
        n_local += 1
        copy.start()
        return copy

    query_copies = [local(q_hbm, q_ref), local(go_hbm, go_ref)]
    weight_copies = [local(wq_hbm, wq_ref), local(wk_hbm, wk_ref), local(wv_hbm, wv_ref)]
    out_copies = []

    for copy in choice_copies:
        copy.wait()
    lanes = lax.broadcasted_iota(jnp.int32, (2, HD), 1)
    for q in range(CHUNK):
        picked = chv_ref[q]
        found = jnp.full((2, HD), TOPK, jnp.int32)
        for n in range(TOPK):
            found = jnp.where(picked[:, n : n + 1] == lanes, n, found)
        names_ref[q] = found
        tm_ref[q, TOPK] = jnp.zeros((BLOCK, 2 * HD), BF16)

    pl.semaphore_wait(barrier, len(partners))
    names_copy = local(names_ref, inv_ref)

    units = [(g, kv) for g in range(2) for kv in range(2)]

    def slot(u, idx):
        g, kv = units[u]
        return kv_bufs[g][kv].at[pl.ds(pl.multiple_of(idx * CHUNK, CHUNK), CHUNK)]

    def put(u, idx, where):
        return plan(slot(u, idx), slot(u, idx), where)

    g_near, g_far, g_core, g_y = {}, {}, {}, {}
    for u in range(4):
        g_y[u] = put(u, c, to_y)
        for n, plane in enumerate((yh, py)):
            first = ctx_at(plane, x, k)
            g_near[u, n] = (put(u, first, to_right), put(u, first, to_left))
            if n == 1:
                g_far[u, n] = put(u, ctx_at(yh, xo, k), to_y)
            elif units[u][1] == 0:
                g_far[u, n] = put(u, ctx_at(plane, xl, k), to_right)
            else:
                g_far[u, n] = put(u, ctx_at(plane, xr, k), to_left)
            g_core[u, n] = [put(u, ctx_at(plane, xx, k), to_core) for xx in (x, xl, xr, xo)]

    def gather_first(u):
        for copy in own_copies[u]:
            copy.wait()
        g_near[u, 0][0].start()
        g_near[u, 0][1].start()
        g_core[u, 0][0].start()

    def gather_over(u):
        g_y[u].start()

    def gather_relay(u, n):
        for side in range(2):
            g_near[u, n][side].wait_recv()
            if n == 0 and units[u][1] == side:
                g_far[u, 0].start()
            g_core[u, n][1 + side].start()

    def gather_y(u):
        g_y[u].wait_recv()
        g_near[u, 1][0].start()
        g_near[u, 1][1].start()
        g_core[u, 1][0].start()

    def gather_far(u, n):
        g_far[u, n].wait_recv()
        if n == 0:
            g_far[u, 1].start()
        g_core[u, n][3].start()

    def gather_end(u):
        for n in range(2):
            for copy in g_core[u, n]:
                copy.wait_recv()

    def each(step, *names):
        for name in names:
            step(*name)

    for u in range(4):
        gather_first(u)
        gather_over(u)
    each(gather_relay, *((u, 0) for u in range(4)))
    each(gather_y, *((u,) for u in range(4)))
    each(gather_far, *((u, 0) for u in range(4)))
    each(gather_relay, (0, 1), (1, 1))
    each(gather_far, (0, 1), (1, 1))
    each(gather_end, (0,), (1,))
    for copy in query_copies:
        copy.wait()
    names_copy.wait()

    base = lax.broadcasted_iota(jnp.int32, (BLOCK, HD), 0) - (
        lax.broadcasted_iota(jnp.int32, (BLOCK, HD), 1) % BLOCK
    )

    def attend(g, q):
        own = c * CHUNK + q
        rows = pl.ds(pl.multiple_of(q * BLOCK, BLOCK), BLOCK)
        qb = jnp.concatenate([q_ref[rows, pl.ds((2 * g + i) * HD, HD)] for i in range(2)], axis=0)
        gb = jnp.concatenate([go_ref[rows, pl.ds((2 * g + i) * HD, HD)] for i in range(2)], axis=0)
        none = jnp.zeros((HD, HD), BF16)
        pair = jnp.concatenate(
            [jnp.concatenate([qb, none], axis=1), jnp.concatenate([none, gb], axis=1)], axis=0
        )
        blocks = [ch_ref[q, g, s] for s in range(TOPK)]
        kc = jnp.concatenate([kv_bufs[g][0][b] for b in blocks], axis=0)
        vc = jnp.concatenate([kv_bufs[g][1][b] for b in blocks], axis=0)
        lines = jnp.concatenate([kc, vc], axis=1)
        products = jnp.concatenate(
            [
                lax.dot_general(lines[:HALF_K], pair, NT, preferred_element_type=F32),
                lax.dot_general(lines[HALF_K:], pair, NT, preferred_element_type=F32),
            ],
            axis=0,
        )
        grad_w = products[:, HD:]
        scores = jnp.concatenate(
            [
                jnp.where(
                    base <= (own - blocks[s]) * BLOCK,
                    products[s * BLOCK : (s + 1) * BLOCK, :HD],
                    -1e30,
                )
                for s in range(TOPK)
            ],
            axis=0,
        )
        top = jnp.max(scores, axis=0, keepdims=True)
        weights = jnp.exp2((scores - top) * EXP2_SCALE)
        weights = weights * (1.0 / jnp.sum(weights, axis=0, keepdims=True))
        low = weights.astype(BF16)
        deltas = jnp.sum(low.astype(F32) * grad_w, axis=0, keepdims=True)
        grad_s = (weights * (grad_w - deltas)).astype(BF16)
        grad_q = SCALE * lax.dot_general(grad_s, kc, TN, preferred_element_type=F32)
        for i in range(2):
            gq_ref[rows, pl.ds((2 * g + i) * HD, HD)] = grad_q[i * BLOCK : (i + 1) * BLOCK].astype(BF16)
        lines = jnp.concatenate([grad_s, low], axis=1)
        term = jnp.concatenate(
            [
                jnp.dot(lines[:HALF_K], pair, preferred_element_type=F32),
                jnp.dot(lines[HALF_K:], pair, preferred_element_type=F32),
            ],
            axis=0,
        )
        for s in range(TOPK):
            part = term[s * BLOCK : (s + 1) * BLOCK]
            tm_ref[q, s, :, :HD] = (SCALE * part[:, :HD]).astype(BF16)
            tm_ref[q, s, :, HD:] = part[:, HD:].astype(BF16)

    def terms(g, plane):
        def body(i, carry):
            for b in range(2 * CHUNK):
                j = (plane * 4 + i) * (2 * CHUNK) + b
                total = tm_ref[0, inv_ref[0, g, j]].astype(F32)
                for q in range(1, CHUNK):
                    total = total + tm_ref[q, inv_ref[q, g, j]].astype(F32)
                total = total.astype(BF16)
                lines = pl.ds((b % CHUNK) * BLOCK, BLOCK)
                t_ref[2 * g, plane, b // CHUNK, i, lines, :] = total[:, :HD]
                t_ref[2 * g + 1, plane, b // CHUNK, i, lines, :] = total[:, HD:]
            return carry

        lax.fori_loop(0, 4, body, 0)

    planes = (py, yh)
    core_sums = {
        (u, n): plan(t_ref.at[u, planes[n], 1 - k], p_ref.at[u, planes[n]], to_core)
        for u in range(4)
        for n in range(2)
    }

    class Sum:
        def __init__(self, way, theirs, mine, bufs, places, ends, over, sender=None):
            self.sender = sender
            begin = len(started)
            self.way, self.theirs, self.mine, self.bufs = way, theirs, mine, bufs
            self.here, right, left, across = places
            self.across = across
            go_right, go_left = ends
            first, far, l0, r0, l1, r1, stage, last = bufs
            self.first = plan(theirs.at[across], first, over)
            self.theirs_right = plan(theirs.at[right], l1, go_right)
            self.theirs_left = plan(theirs.at[left], r1, go_left)
            self.over = plan(stage, last, over)
            if sender is not None:
                one_way.update(range(begin, len(started)))
            self.far = plan(mine.at[across], far, go_right if way == 0 else go_left)
            self.mine_right = plan(mine.at[right], l0, go_right)
            self.mine_left = plan(mine.at[left], r0, go_left)
            self.relayed, self.direct = (
                (self.mine_right, self.mine_left) if way == 0 else (self.mine_left, self.mine_right)
            )
            self.relay_at = right if way == 0 else left

        def gate(self, sends, action):
            if self.sender is None:
                action()
            else:
                pl.when(self.sender if sends else jnp.logical_not(self.sender))(action)

        def start_first(self):
            self.gate(True, self.first.start)

        def start_near(self):
            def action():
                self.theirs_right.start()
                self.theirs_left.start()

            self.gate(True, action)

        def start_theirs(self):
            self.start_first()
            self.start_near()

        def start_mine(self):
            self.direct.start()

        def add(self, i, buf):
            self.mine[i] = (self.mine[i].astype(F32) + buf[...].astype(F32)).astype(BF16)

        def far_now(self):
            self.gate(True, self.far.start)

        def go_far(self):
            def action():
                self.first.wait_recv()
                self.add(self.across, self.bufs[0])
                self.far.start()

            self.gate(False, action)

        def cross(self):
            def action():
                _, _, _, _, l1, r1, stage, _ = self.bufs
                self.theirs_right.wait_recv()
                self.theirs_left.wait_recv()
                total = self.theirs[self.here].astype(F32) + l1[...].astype(F32) + r1[...].astype(F32)
                stage[...] = total.astype(BF16)
                self.over.start()

            self.gate(True, action)

        def relay(self):
            self.far.wait_recv()
            self.add(self.relay_at, self.bufs[1])
            self.relayed.start()

        def end(self):
            _, _, l0, r0, _, _, _, last = self.bufs
            self.mine_right.wait_recv()
            self.mine_left.wait_recv()
            total = self.mine[self.here].astype(F32) + l0[...].astype(F32) + r0[...].astype(F32)
            self.gate(False, self.over.wait_recv)
            return total + last[...].astype(F32)

    later = yh == 1

    @pl.when(later)
    def _():
        xy_ref[...] = jnp.zeros(xy_ref.shape, BF16)

    x_sums = {
        (u, e): Sum(
            u % 2, s_ref.at[u, e, py], s_ref.at[u, e, yh],
            (xa_ref.at[u, e], xf_ref.at[u, e], xl_ref.at[u, e, 0], xr_ref.at[u, e, 0],
             xl_ref.at[u, e, 1], xr_ref.at[u, e, 1], xs_ref.at[u, e], xy_ref.at[u, e]),
            (x, xr, xl, xo), (to_right, to_left), to_y, later,
        )
        for u in range(4)
        for e in range(2)
    }

    def core_sum(u, n):
        plane = planes[n]
        core_sums[u, n].wait_recv()
        for e in range(2):
            half = pl.ds(e * HD, HD)
            for xx in range(4):
                s_ref[u, e, plane, xx] = (
                    t_ref[u, plane, k, xx, half, :].astype(F32) + p_ref[u, plane, xx, half, :].astype(F32)
                ).astype(BF16)

    def sum_end(u, e):
        g, kv = units[u]
        (gk_ref, gv_ref)[kv][pl.ds(e * HD, HD), pl.ds(g * HD, HD)] = x_sums[u, e].end().astype(BF16)

    def do(names, *steps):
        for step in steps:
            for name in names:
                getattr(x_sums[name], step)()

    def core_start(g, n):
        core_sums[2 * g, n].start()
        core_sums[2 * g + 1, n].start()

    LOW = [[(0, e), (1, e)] for e in range(2)]
    HIGH = [[(2, e), (3, e)] for e in range(2)]
    hooks = {
        (0, 1): lambda: (
            each(gather_relay, (2, 1), (3, 1)),
            each(gather_far, (2, 1), (3, 1)),
        ),
        (1, 1): lambda: (
            each(core_sum, (0, 0), (1, 0)),
            do(LOW[0] + LOW[1], "start_theirs"),
            each(core_sum, (0, 1), (1, 1)),
            do(LOW[0] + LOW[1], "far_now", "start_mine"),
        ),
    }
    for g in range(2):
        if g == 1:
            each(gather_end, (2,), (3,))

        def step(q, carry, g=g):
            for (gg, at), action in hooks.items():
                if gg == g:
                    pl.when(q == at)(lambda action=action: (action(), None)[1])
            attend(g, 2 * q)
            attend(g, 2 * q + 1)
            return carry

        lax.fori_loop(0, CHUNK // 2, step, 0)
        if g == 1:
            out_copies.append(local(gq_ref, gq_hbm))
        for n in range(2):
            terms(g, planes[n])
            core_start(g, n)
    do(LOW[0] + LOW[1], "go_far")

    for copy in weight_copies:
        copy.wait()

    def query_part(i, carry):
        rows = pl.ds(pl.multiple_of(i * OUT_W, OUT_W), OUT_W)
        acc_ref[rows, :] = lax.dot_general(wq_ref[rows, :], gq_ref[...], NT, preferred_element_type=F32)
        return carry

    each(core_sum, (2, 0), (3, 0))
    do(HIGH[0], "start_theirs")
    do(HIGH[1], "start_first")
    each(core_sum, (2, 1), (3, 1))
    do(HIGH[0], "far_now")
    do(LOW[0], "cross")
    lax.fori_loop(0, 4, query_part, 0)
    do(HIGH[0], "go_far")
    do(LOW[0] + LOW[1], "relay")
    lax.fori_loop(4, 5, query_part, 0)
    do(HIGH[0], "start_mine", "cross")
    do(LOW[1], "cross")
    do(HIGH[1][:1], "start_near")
    lax.fori_loop(5, 8, query_part, 0)
    do(HIGH[0], "relay")
    do(HIGH[1][1:], "start_near")
    do(HIGH[1], "far_now", "go_far", "start_mine")
    each(sum_end, *((u, 0) for u in range(4)))

    z_places = (z, zr, zl, zo)
    z_sums = {
        (e, w): Sum(
            w, pt_ref.at[e, w, 1 - yl], pt_ref.at[e, w, yl],
            (za_ref.at[e, w], zf_ref.at[e, w], zl_ref.at[e, w, 0], zr_ref.at[e, w, 0],
             zl_ref.at[e, w, 1], zr_ref.at[e, w, 1], zs_ref.at[e, w], zy_ref.at[e, w]),
            z_places, (to_zr, to_zl), to_yl,
        )
        for e in range(2)
        for w in range(2)
    }

    def term_chunk(e, side, zz):
        i = zz * 2 + side
        rows = pl.ds(pl.multiple_of(i * OUT_W, OUT_W), OUT_W)
        half = pl.ds(e * HD, HD)
        out = acc_ref[rows, half]
        out = out + lax.dot_general(wk_ref[rows, :], gk_ref[half, :], NT, preferred_element_type=F32)
        out = out + lax.dot_general(wv_ref[rows, :], gv_ref[half, :], NT, preferred_element_type=F32)
        out = out.astype(BF16)
        for w in range(2):
            pt_ref[e, w, side, zz] = out[w * HALF_W : (w + 1) * HALF_W]

    def both(e, step):
        for w in range(2):
            step(z_sums[e, w])

    def send_first(e):
        term_chunk(e, 1 - yl, zo)
        both(e, lambda t: t.first.start())

    def send_near(e):
        term_chunk(e, 1 - yl, zr)
        both(e, lambda t: t.theirs_right.start())
        term_chunk(e, 1 - yl, zl)
        both(e, lambda t: t.theirs_left.start())

    def own_chunks(e):
        for zz in (zo, zl, zr):
            term_chunk(e, yl, zz)

    def last_chunks(e):
        term_chunk(e, 1 - yl, z)
        term_chunk(e, yl, z)

    def z_end(e):
        for w in range(2):
            part = (pl.ds(w * HALF_W, HALF_W), pl.ds(e * HD, HD))
            gi_ref[part] = z_sums[e, w].end().astype(BF16)
            out_copies.append(local(gi_ref.at[part], gi_hbm.at[part]))

    do(HIGH[1], "cross")
    send_first(0)
    do(HIGH[1], "relay")
    send_near(0)
    own_chunks(0)
    last_chunks(0)
    both(0, lambda t: (t.go_far(), t.start_mine()))
    each(sum_end, *((u, 1) for u in range(4)))
    out_copies.append(local(gk_ref, gk_hbm))
    out_copies.append(local(gv_ref, gv_hbm))
    send_first(1)
    send_near(1)
    own_chunks(1)
    last_chunks(1)
    both(0, lambda t: t.cross())
    both(1, lambda t: (t.go_far(), t.start_mine()))
    both(0, lambda t: t.relay())
    both(1, lambda t: t.cross())
    both(1, lambda t: t.relay())
    z_end(0)
    z_end(1)

    for copy in out_copies:
        copy.wait()
    for i, copy in enumerate(started):
        if i in one_way:
            pl.when(later)(copy.wait_send)
        else:
            copy.wait_send()


def write_out(*refs):
    sources, targets, held, sem = refs[:4], refs[4:8], refs[8:12], refs[12]
    loads = [pltpu.make_async_copy(sources[i], held[i], sem.at[i]) for i in range(4)]
    stores = [pltpu.make_async_copy(held[i], targets[i], sem.at[4 + i]) for i in range(4)]
    for copy in loads:
        copy.start()
    for load, store in zip(loads, stores):
        load.wait()
        store.start()
    for copy in stores:
        copy.wait()


def body(queries, keys, values, grad_out, chosen, w_query, w_key, w_value):
    hbm = pl.BlockSpec(memory_space=pl.ANY)
    shape = jax.ShapeDtypeStruct
    buf = lambda *dims: pltpu.VMEM(dims, BF16)
    chunk = (ROWS, HD)
    zc = (2, HALF_W, HD)
    outs = pl.pallas_call(
        kernel,
        out_shape=(
            shape((ROWS, 512), BF16),
            shape((ROWS, 256), BF16),
            shape((ROWS, 256), BF16),
            shape((OUT_W, ROWS), BF16),
        ),
        in_specs=[hbm] * 8,
        out_specs=(hbm,) * 4,
        scratch_shapes=[
            buf(64, BLOCK, HD), buf(64, BLOCK, HD), buf(64, BLOCK, HD), buf(64, BLOCK, HD),
            buf(ROWS, 512), buf(ROWS, 512), buf(ROWS, 512), buf(ROWS, 256), buf(ROWS, 256), buf(OUT_W, ROWS),
            buf(CHUNK, TOPK + 1, BLOCK, 2 * HD),
            pltpu.SMEM((CHUNK, 2, TOPK), jnp.int32), pltpu.VMEM((CHUNK, 2, TOPK), jnp.int32),
            pltpu.VMEM((CHUNK, 2, HD), jnp.int32), pltpu.SMEM((CHUNK, 2, HD), jnp.int32),
            buf(4, 2, 2, 4, *chunk), buf(4, 2, 4, *chunk), buf(4, 2, 2, 4, HD, HD),
            buf(4, 2, HD, HD), buf(4, 2, HD, HD), buf(4, 2, 2, HD, HD), buf(4, 2, 2, HD, HD), buf(4, 2, HD, HD), buf(4, 2, HD, HD),
            buf(4608, 512), buf(4608, 256), buf(4608, 256), pltpu.VMEM((4608, ROWS), F32),
            buf(2, 2, 2, 4, HALF_W, HD), buf(2, *zc), buf(2, *zc),
            buf(2, 2, 2, HALF_W, HD), buf(2, 2, 2, HALF_W, HD), buf(2, *zc), buf(2, *zc),
            pltpu.SemaphoreType.DMA((N_COPIES,)),
            pltpu.SemaphoreType.DMA((N_COPIES,)),
            pltpu.SemaphoreType.DMA((32,)),
        ],
        compiler_params=pltpu.CompilerParams(
            collective_id=0, has_side_effects=True, vmem_limit_bytes=60 * 1024 * 1024
        ),
    )(queries, grad_out, keys, values, chosen, w_query, w_key, w_value)
    grad_queries, grad_keys, grad_values, grad_input = pl.pallas_call(
        write_out,
        out_shape=tuple(shape(o.shape, o.dtype) for o in outs),
        in_specs=[hbm] * 4,
        out_specs=(hbm,) * 4,
        scratch_shapes=[pltpu.VMEM(o.shape, o.dtype) for o in outs] + [pltpu.SemaphoreType.DMA((8,))],
        compiler_params=pltpu.CompilerParams(vmem_limit_bytes=60 * 1024 * 1024),
    )(*outs)
    return grad_queries, grad_keys, grad_values, grad_input.T


def solution(mesh):
    both = P("ctx", "head")
    return jax.shard_map(
        body,
        mesh=mesh,
        in_specs=(both, both, both, both, P("ctx", "head", None)) + (P(None, "head"),) * 3,
        out_specs=(both, both, both, both),
        check_vma=False,
    )
```
